32 devices in a mesh: loop: 8 (over z, x), rep: 4 (over y, core).
Axes of the slice: x: 2, y: 2, z: 4, core: 2. Of those that a mesh axis runs over, the one named last changes fastest.
Arguments:
- features: float32 [4096, 128], P('loop'), may hold values from -6 to 6
- weight: float32 [128, 256], replicated, may hold values from -0.5 to 0.5
- bias: float32 [256], replicated, may hold values from -3 to 3
- tile_values: float32 [512, 128, 128], P(('loop', 'rep')), may hold values from -0.125 to 0.125
- tile_rows: int32 [512], P(('loop', 'rep')), may hold values from 0 to 31, as said below
- tile_cols: int32 [512], P(('loop', 'rep')), may hold values from 0 to 31, as said below
- tile_count: int32 [32], P(('loop', 'rep')), may hold values from 1 to 16, as said below
- cotangent: float32 [4096, 256], P('loop'), may hold values from -0.6 to 0.6
Outputs:
- output: float32 [4096, 256], P('loop')
- grad_features: float32 [4096, 128], P('loop')
- grad_weight: float32 [128, 256], replicated
- grad_bias: float32 [256], replicated
The draws below stay inside these ranges and needn't reach their ends.
Inputs may be any that keep to these rules, and one draw needn't show every extreme that they name: `tile_rows`: every slot of a device at loop index l names a row block from l * 4 to (l + 1) * 4 - 1. `tile_cols`: for every loop index m, the live slots of one device name at most 2 different column blocks from m * 4 to (m + 1) * 4 - 1; for every loop index some device names exactly 2 of one such range. `tile_count`: for every loop index some device has all 16 slots live.
All inputs are finite; a program needn't handle non-finite values.
Results may differ from the reference program's by a relative error of at most 0.0001.
Values sent between devices are 32-bit elements; how exact they have to be, the bound alone decides.
No kernel may reach another device: no remote copies, remote signals or barrier semaphores. Data moves between devices by JAX's collectives and lax.ppermute only.
A program may use at most 64 MiB of HBM per device.

```python
import jax
import jax.numpy as jnp
from jax import lax

F_IN = 128
F_OUT = 256
TILE = 128
COL_CAP = 2
BLK_DEV = 4
TILE_DEV = 16
NODES = 4096
TILES = 512
N_LOOP = 8
N_REP = 4


def tile_layout(key):
    devices = N_LOOP * N_REP
    keys = jax.random.split(jax.random.fold_in(key, 7), 8)
    slot_ids = jnp.arange(TILE_DEV, dtype=jnp.int32)[None, :]
    target_loop = jax.random.randint(keys[0], (devices, TILE_DEV), 0, N_LOOP)
    first_target = jax.random.randint(keys[1], (devices,), 0, N_LOOP)
    target_loop = jnp.where(slot_ids < COL_CAP, first_target[:, None], target_loop)
    which = jax.random.randint(keys[2], (devices, TILE_DEV), 0, COL_CAP)
    which = jnp.where(slot_ids < COL_CAP, slot_ids, which)
    scores = jax.random.randint(keys[3], (devices, N_LOOP, BLK_DEV), 0, 4096) * BLK_DEV
    scores = scores + jnp.arange(BLK_DEV, dtype=jnp.int32)
    column_sets = jnp.argsort(scores, axis=2, stable=True)[:, :, :COL_CAP].astype(jnp.int32)
    flat_sets = column_sets.reshape(devices, N_LOOP * COL_CAP)
    local_col = jnp.take_along_axis(flat_sets, target_loop * COL_CAP + which, axis=1)
    col_ids = target_loop * BLK_DEV + local_col
    device_loop = jnp.arange(devices, dtype=jnp.int32) // N_REP
    favoured = jax.random.randint(keys[4], (N_LOOP,), 0, BLK_DEV)[device_loop]
    row_draw = jax.random.randint(keys[5], (devices, TILE_DEV), 0, 2 * BLK_DEV)
    local_row = jnp.where(row_draw < BLK_DEV, row_draw, favoured[:, None])
    row_ids = device_loop[:, None] * BLK_DEV + local_row
    counts = jax.random.randint(keys[6], (N_LOOP, N_REP), 1, TILE_DEV + 1)
    full_rep = jax.random.randint(keys[7], (N_LOOP,), 0, N_REP)
    counts = jnp.where(jnp.arange(N_REP)[None, :] == full_rep[:, None], TILE_DEV, counts)
    return (row_ids.reshape(-1).astype(jnp.int32), col_ids.reshape(-1).astype(jnp.int32), counts.reshape(-1).astype(jnp.int32))


def draw_tile_rows(key, part):
    return tile_layout(key)[0]


def draw_tile_cols(key, part):
    return tile_layout(key)[1]


def draw_tile_count(key, part):
    return tile_layout(key)[2]


def block_scale(stream_key, shape, cuts, smallest, top_value):
    loudness, own = 1.0, jax.random.fold_in(stream_key, 6)
    for axis_at, shards_of in cuts:
        heights = jnp.exp(jax.random.uniform(jax.random.fold_in(own, axis_at), (shards_of,), jnp.float32, smallest / len(cuts), top_value / len(cuts)))
        loudness = loudness * jnp.repeat(heights, shape[axis_at] // shards_of).reshape([-1 if axis == axis_at else 1 for axis in range(len(shape))])
    return loudness


def gaussian(rng, extent, deviation, most, cuts=(), kind=jnp.bfloat16):
    factor_of = block_scale(rng, extent, cuts, -0.22, 0.18) if cuts else 1.0
    drawn = jax.random.normal(rng, extent, jnp.float32) * deviation * factor_of
    return jnp.minimum(jnp.maximum(drawn, -most), most).astype(kind)


def setup_inputs(seed: int = 0) -> dict:
    key_of = jax.random.split(jax.random.key(seed), 9)
    features = gaussian(key_of[0], (NODES, F_IN), 1.0, 6.0, ((0, 8),), jnp.float32)
    weight = gaussian(key_of[1], (F_IN, F_OUT), F_IN ** -0.5, 0.5, (), jnp.float32)
    bias = gaussian(key_of[2], (F_OUT,), 0.5, 3.0, (), jnp.float32)
    tile_values = gaussian(key_of[3], (TILES, TILE, TILE), (TILE * 16) ** -0.5, 0.125, ((0, 32),), jnp.float32)
    tile_rows = draw_tile_rows(jax.random.fold_in(key_of[8], 71), 0)
    tile_cols = draw_tile_cols(jax.random.fold_in(key_of[8], 71), 0)
    tile_count = draw_tile_count(jax.random.fold_in(key_of[8], 71), 0)
    cotangent = gaussian(key_of[7], (NODES, F_OUT), 0.1, 0.6, ((0, 8),), jnp.float32)
    return dict(features=features, weight=weight, bias=bias, tile_values=tile_values, tile_rows=tile_rows, tile_cols=tile_cols, tile_count=tile_count, cotangent=cotangent)


def block_product(tile_values, tile_rows, tile_cols, tile_count, dense_in, transpose):
    tile_side = tile_values.shape[1]
    nblocks = dense_in.shape[0] // tile_side
    width = dense_in.shape[1]
    blocks = dense_in.reshape(nblocks, tile_side, width)
    devices = tile_count.shape[0]
    values = tile_values.reshape(devices, -1, tile_side, tile_side)
    row_ids = tile_rows.reshape(devices, -1).astype(jnp.int32)
    col_ids = tile_cols.reshape(devices, -1).astype(jnp.int32)
    slot_ids = jnp.arange(values.shape[1], dtype=jnp.int32)
    live_slot = (slot_ids[None, :] < tile_count[:, None].astype(jnp.int32)).astype(jnp.float32)

    def step(running, portion):
        vals, rows_here, cols_here, alive = portion
        if transpose:
            source, target, pattern = rows_here, cols_here, "kji,kjf->kif"
        else:
            source, target, pattern = cols_here, rows_here, "kij,kjf->kif"
        product = jnp.einsum(pattern, vals, blocks[source], precision=lax.Precision.HIGHEST)
        product = product * alive[:, None, None]
        return running.at[target].add(product), None

    initial = jnp.zeros((nblocks, tile_side, width), jnp.float32)
    summed, _ = lax.scan(step, initial, (values, row_ids, col_ids, live_slot))
    return summed.reshape(nblocks * tile_side, width)


def reference(features, weight, bias, tile_values, tile_rows, tile_cols, tile_count, cotangent):
    aggregated = block_product(tile_values, tile_rows, tile_cols, tile_count, features, False)
    preactive = jnp.dot(aggregated, weight, precision=lax.Precision.HIGHEST) + bias
    logistic = jax.nn.sigmoid(preactive)
    output = preactive * logistic
    gradient = cotangent * logistic * (1.0 + preactive * (1.0 - logistic))
    grad_weight = jnp.dot(aggregated.T, gradient, precision=lax.Precision.HIGHEST)
    grad_bias = jnp.sum(gradient, axis=0)
    spread = jnp.dot(gradient, weight.T, precision=lax.Precision.HIGHEST)
    grad_features = block_product(tile_values, tile_rows, tile_cols, tile_count, spread, True)
    return output, grad_features, grad_weight, grad_bias
```

```python
import functools

import jax
import jax.numpy as jnp
from jax import lax
from jax.experimental import pallas as pl
from jax.experimental.pallas import tpu as pltpu
from jax.sharding import PartitionSpec as P

LANES = 128
PAD = 8
F32 = jnp.float32
BF16 = jnp.bfloat16
VMEM = pl.BlockSpec(memory_space=pltpu.VMEM)
SMEM = pl.BlockSpec(memory_space=pltpu.SMEM)


def halves(x):
    high = x.astype(BF16).astype(F32)
    return high, x - high


def dot3(a, b, dims=(((1,), (0,)), ((), ()))):
    ah, al = halves(a)
    bh, bl = halves(b)
    ah, al, bh, bl = (v.astype(BF16) for v in (ah, al, bh, bl))
    dot = functools.partial(lax.dot_general, dimension_numbers=dims, preferred_element_type=F32)
    return dot(ah, bh) + dot(ah, bl) + dot(al, bh)


def call(kernel, out_shapes, in_specs, scratch, flops, moved, name, limit=24):
    return pl.pallas_call(
        kernel,
        out_shape=[jax.ShapeDtypeStruct(s, F32) for s in out_shapes],
        in_specs=in_specs,
        out_specs=[VMEM] * len(out_shapes),
        scratch_shapes=scratch,
        compiler_params=pltpu.CompilerParams(vmem_limit_bytes=limit << 20),
        cost_estimate=pl.CostEstimate(flops=flops, bytes_accessed=moved, transcendentals=0),
        name=name,
    )


def pack_kernel(reps, part, here, count, tiles, meta, *refs):
    outs, turned = refs[:reps], refs[reps]
    slots, side = tiles.shape[0], tiles.shape[1]
    for s in range(slots):
        turned[s] = jnp.where(s < count[0], tiles[s].T, jnp.zeros((side, side), F32))
    for d in range(reps):
        start = pl.multiple_of((here[0] ^ d) * part, 8)
        for s in range(slots):
            outs[d][pl.ds(s * part, part), :] = turned[s, pl.ds(start, part), :]
        outs[d][pl.ds(slots * part, PAD), :] = meta[...]


def forward_kernel(reps, loops, blocks, part, slots, here, rows, cols, *refs):
    tiles, feats = refs[:reps], refs[reps : reps + loops]
    send, keep, rhs, acc = refs[reps + loops :]
    side = acc.shape[0] // blocks
    for k in range(loops):
        for b in range(blocks):
            high, low = halves(feats[k][pl.ds(b * part, part), :])
            rhs[k * blocks + b] = jnp.concatenate([high, low, high], axis=0).astype(BF16)
    acc[...] = jnp.zeros_like(acc)
    for d in range(reps):

        def slot(s, carry, d=d):
            high, low = halves(tiles[d][pl.ds(pl.multiple_of(s * part, 8), part), :])
            lhs = jnp.concatenate([high, high, low], axis=0).astype(BF16)
            product = lax.dot_general(
                lhs, rhs[cols[d, s]], (((0,), (0,)), ((), ())), preferred_element_type=F32
            )
            at = pl.ds(pl.multiple_of(rows[d, s] * side, 8), side)
            acc[at, :] = acc[at, :] + product
            return carry

        lax.fori_loop(0, slots, slot, 0, unroll=4)
    half = acc.shape[0] // 2
    core = here[0] & 1
    keep[...] = acc[pl.ds(pl.multiple_of(core * half, 8), half), :]
    send[...] = acc[pl.ds(pl.multiple_of((1 - core) * half, 8), half), :]


def backward_kernel(reps, loops, blocks, part, slots, here, rows, cols, *refs):
    tiles = refs[:reps]
    mine, other, weight, bias, cotangent, output, send, keep = refs[reps : reps + 8]
    agg, turned, grads, right, products, acc = refs[reps + 8 :]
    total, width = agg.shape
    half, side = total // 2, total // blocks
    wide = output.shape[1]
    core = here[0] & 1
    agg[pl.ds(pl.multiple_of(core * half, 8), half), :] = mine[...]
    agg[pl.ds(pl.multiple_of((1 - core) * half, 8), half), :] = other[...]
    w = weight[...]
    for b in range(blocks):
        at = pl.ds(b * side, side)
        a = agg[at, :]
        turned[:, at] = a.T
        pre = dot3(a, w) + bias[...]
        gate = jax.nn.sigmoid(pre)
        output[at, :] = pre * gate
        gradient = cotangent[at, :] * gate * (1.0 + pre * (1.0 - gate))
        grads[at, :] = gradient
        spread = dot3(gradient, w, (((1,), (1,)), ((), ())))
        high, low = halves(spread)
        right[:, pl.ds(b * side, side)] = jnp.concatenate([high, low, high], axis=0).astype(BF16)
    g = grads[...]
    piece = width // reps
    grad_weight = dot3(turned[pl.ds(pl.multiple_of(here[0] * piece, 8), piece), :], g)
    grad_bias = jnp.sum(g, axis=0, keepdims=True)
    groups = wide // LANES
    acc[...] = jnp.zeros_like(acc)
    for d in range(reps):
        high, low = halves(tiles[d][pl.ds(0, slots * part), :])
        left = jnp.concatenate([high, high, low], axis=1).astype(BF16)
        products[...] = jnp.dot(left, right[...], preferred_element_type=F32)

        def slot(s, carry, d=d):
            lane = pl.multiple_of(rows[d, s] * LANES, LANES)
            value = products[pl.ds(pl.multiple_of(s * part, 8), part), pl.ds(lane, LANES)]
            at = pl.ds(pl.multiple_of(cols[d, s] * part, 8), part)
            acc[at, :] = acc[at, :] + value
            return carry

        lax.fori_loop(0, slots, slot, 0, unroll=4)
    size = blocks * part
    for k in range(loops):
        target = send if k & 1 else keep
        target[pl.ds((k // 2) * size, size), :] = acc[pl.ds(k * size, size), :]
    base = (loops // 2) * size
    for target in (send, keep):
        for q in range(groups):
            target[pl.ds(base + q * piece, piece), :] = grad_weight[:, q * LANES : (q + 1) * LANES]
        tail = [grad_bias[:, q * LANES : (q + 1) * LANES] for q in range(groups)]
        tail.append(jnp.zeros((PAD - groups, LANES), F32))
        target[pl.ds(base + groups * piece, PAD), :] = jnp.concatenate(tail, axis=0)


def add_kernel(count, size, extra, mine, theirs, *outs):
    for k in range(count):
        at = pl.ds(k * size, size)
        value = mine[at, :] + theirs[at, :]
        if count == 1:
            outs[0][at, :] = value
        else:
            outs[1 - (k & 1)][pl.ds((k // 2) * size, size), :] = value
    value = mine[pl.ds(count * size, extra), :] + theirs[pl.ds(count * size, extra), :]
    for out in outs:
        out[pl.ds(max(count // 2, 1) * size, extra), :] = value


def final_kernel(reps, blocks, part, piece, here, *refs):
    parts = refs[:reps]
    grad_features, grad_weight, grad_bias = refs[reps:]
    side = grad_features.shape[0] // blocks
    groups = grad_weight.shape[1] // LANES
    base = blocks * part
    for d in range(reps):
        q = here[0] ^ d
        for b in range(blocks):
            at = pl.ds(pl.multiple_of(b * side + q * part, 8), part)
            grad_features[at, :] = parts[d][pl.ds(b * part, part), :]
        at = pl.ds(pl.multiple_of(q * piece, 8), piece)
        for g in range(groups):
            grad_weight[at, pl.ds(g * LANES, LANES)] = parts[d][pl.ds(base + g * piece, piece), :]
    for g in range(groups):
        row = parts[0][pl.ds(base + groups * piece + g, 1), :]
        grad_bias[:, pl.ds(g * LANES, LANES)] = row


def per_device(features, weight, bias, tile_values, tile_rows, tile_cols, tile_count, cotangent):
    loops, reps = lax.axis_size("loop"), lax.axis_size("rep")
    loop_at, rep_at = lax.axis_index("loop"), lax.axis_index("rep")
    slots, side = tile_values.shape[0], tile_values.shape[1]
    total, width = features.shape
    wide = weight.shape[1]
    blocks = total // side
    part, piece, groups = side // reps, width // reps, wide // LANES
    size = blocks * part
    extra = groups * piece + PAD
    here = rep_at.astype(jnp.int32).reshape(1)

    def swap(x, axis, bit):
        n = lax.axis_size(axis)
        return lax.ppermute(x, axis, [(i, i ^ bit) for i in range(n)])

    own = lax.dynamic_index_in_dim(
        features.reshape(blocks, reps, part, width), rep_at, 1, keepdims=False
    ).reshape(size, width)
    feats = {0: own}
    bit = loops // 2
    while bit:
        for k in list(feats):
            feats[k | bit] = swap(feats[k], "loop", bit)
        bit //= 2

    local_rows = jnp.clip(tile_rows - loop_at * blocks, 0, blocks - 1)
    place = ((tile_cols // blocks) ^ loop_at) * blocks + tile_cols % blocks
    meta = jnp.pad(
        jnp.stack([local_rows, place]).astype(F32), ((0, PAD - 2), (0, LANES - slots))
    )
    chunks = call(
        functools.partial(pack_kernel, reps, part),
        [(slots * part + PAD, side)] * reps,
        [SMEM, SMEM, VMEM, VMEM],
        [pltpu.VMEM((slots, side, side), F32)],
        0,
        2 * tile_values.size * 4,
        "pack",
    )(here, tile_count, tile_values, meta)
    tiles = [chunks[0]] + [swap(chunks[d], "rep", d) for d in range(1, reps)]
    index = jnp.stack([t[slots * part : slots * part + 2, :slots] for t in tiles]).astype(jnp.int32)
    rows, cols = index[:, 0], index[:, 1]

    count = reps * slots
    send, keep = call(
        functools.partial(forward_kernel, reps, loops, blocks, part, slots),
        [(total // 2, width)] * 2,
        [SMEM] * 3 + [VMEM] * (reps + loops),
        [
            pltpu.VMEM((loops * blocks, 3 * part, width), BF16),
            pltpu.VMEM((total, width), F32),
        ],
        2 * count * part * side * width * 3,
        4 << 20,
        "forward",
    )(here, rows, cols, *tiles, *[feats[k] for k in range(loops)])
    mine = keep + swap(send, "rep", 1)
    bit = 2
    while bit < reps:
        mine = mine + swap(mine, "rep", bit)
        bit *= 2
    other = swap(mine, "rep", 1)

    shape = ((loops // 2) * size + extra, width)
    output, send, keep = call(
        functools.partial(backward_kernel, reps, loops, blocks, part, slots),
        [(total, wide), shape, shape],
        [SMEM] * 3 + [VMEM] * (reps + 5),
        [
            pltpu.VMEM((total, width), F32),
            pltpu.VMEM((width, total), F32),
            pltpu.VMEM((total, wide), F32),
            pltpu.VMEM((3 * width, total), BF16),
            pltpu.VMEM((slots * part, blocks * width), F32),
            pltpu.VMEM((loops * size, width), F32),
        ],
        2 * count * part * side * width * blocks * 3,
        4 << 20,
        "backward",
        limit=32,
    )(here, rows, cols, *tiles, mine, other, weight, bias.reshape(1, wide), cotangent)

    bit, left = 1, loops // 2
    while left:
        shape = (max(left // 2, 1) * size + extra, width)
        summed = call(
            functools.partial(add_kernel, left, size, extra),
            [shape] * (1 if left == 1 else 2),
            [VMEM] * 2,
            [],
            left * size * width,
            3 * left * size * width * 4,
            "add",
        )(keep, swap(send, "loop", bit))
        if left > 1:
            send, keep = summed
        else:
            keep = summed[0]
        bit, left = bit * 2, left // 2

    parts = {0: keep}
    bit = reps // 2
    while bit:
        for k in list(parts):
            parts[k | bit] = swap(parts[k], "rep", bit)
        bit //= 2
    grad_features, grad_weight, grad_bias = call(
        functools.partial(final_kernel, reps, blocks, part, piece),
        [(total, width), (width, wide), (1, wide)],
        [SMEM] + [VMEM] * reps,
        [],
        0,
        2 * total * width * 4,
        "final",
    )(here, *[parts[d] for d in range(reps)])
    return (output, grad_features, grad_weight, grad_bias.reshape(wide))


def solution(mesh):
    return jax.shard_map(
        per_device,
        mesh=mesh,
        in_specs=(
            P("loop", None),
            P(),
            P(),
            P(("loop", "rep"), None, None),
            P(("loop", "rep")),
            P(("loop", "rep")),
            P(("loop", "rep")),
            P("loop", None),
        ),
        out_specs=(P("loop", None), P("loop", None), P(), P()),
        check_vma=False,
    )
```

```python
import functools

import jax
import jax.numpy as jnp
from jax import lax
from jax.experimental import pallas as pl
from jax.experimental.pallas import tpu as pltpu
from jax.sharding import PartitionSpec as P

LANES = 128
PAD = 8
F32 = jnp.float32
BF16 = jnp.bfloat16
VMEM = pl.BlockSpec(memory_space=pltpu.VMEM)
SMEM = pl.BlockSpec(memory_space=pltpu.SMEM)
HBM = pl.BlockSpec(memory_space=pltpu.HBM)


def halves(x):
    high = x.astype(BF16).astype(F32)
    return high, x - high


def dot3(a, b, dims=(((1,), (0,)), ((), ()))):
    ah, al = halves(a)
    bh, bl = halves(b)
    ah, al, bh, bl = (v.astype(BF16) for v in (ah, al, bh, bl))
    dot = functools.partial(lax.dot_general, dimension_numbers=dims, preferred_element_type=F32)
    return dot(ah, bh) + dot(ah, bl) + dot(al, bh)


def call(kernel, out_shapes, in_specs, scratch, flops, moved, name, limit=24):
    return pl.pallas_call(
        kernel,
        out_shape=[
            jax.ShapeDtypeStruct(*(s if isinstance(s[0], tuple) else (s, F32))) for s in out_shapes
        ],
        in_specs=in_specs,
        out_specs=[VMEM] * len(out_shapes),
        scratch_shapes=scratch,
        compiler_params=pltpu.CompilerParams(vmem_limit_bytes=limit << 20),
        cost_estimate=pl.CostEstimate(flops=flops, bytes_accessed=moved, transcendentals=0),
        name=name,
    )


def pack_kernel(reps, blocks, part, rep_at, at_loop, count, features, tiles, rows, cols, *refs):
    own, outs = refs[0], refs[1 : 1 + reps]
    held, turned, row_ids, col_ids, sem = refs[1 + reps :]
    here, loop_at = rep_at[0], at_loop[0]
    slots, side = tiles.shape[0], tiles.shape[1]
    chunks = sem.shape[0] - 2 - blocks
    step = slots // chunks
    small = [
        pltpu.make_async_copy(source, target, sem.at[n])
        for n, (source, target) in enumerate([(rows, row_ids), (cols, col_ids)])
    ]
    large = [
        pltpu.make_async_copy(
            tiles.at[pl.ds(n * step, step)], held.at[pl.ds(n * step, step)], sem.at[2 + n]
        )
        for n in range(chunks)
    ]
    pieces = [
        pltpu.make_async_copy(
            features.at[pl.ds(pl.multiple_of(b * side + here * part, 8), part), :],
            own.at[pl.ds(b * part, part), :],
            sem.at[2 + chunks + b],
        )
        for b in range(blocks)
    ]
    for copy in small + large + pieces:
        copy.start()
    for copy in small:
        copy.wait()
    local_rows = row_ids[...] - loop_at * blocks
    shift = blocks.bit_length() - 1
    column = (((col_ids[...] >> shift) ^ loop_at) << shift) | (col_ids[...] & (blocks - 1))
    meta = jnp.concatenate([local_rows, column], axis=0).astype(F32)
    for d in range(reps):
        outs[d][pl.ds(slots * part, 2), pl.ds(0, slots)] = meta
    alive = count[0]
    for n in range(chunks):
        large[n].wait()
        for s in range(n * step, (n + 1) * step):
            turned[s] = jnp.where(s < alive, held[s].T, jnp.zeros((side, side), F32))
            for d in range(reps):
                start = pl.multiple_of((here ^ d) * part, 8)
                outs[d][pl.ds(s * part, part), :] = turned[s, pl.ds(start, part), :]
    for copy in pieces:
        copy.wait()


def build_kernel(reps, blocks, part, slots, *refs):
    tiles = refs[:reps]
    high_out, low_out, dense, place_vector, place, sem = refs[-6:]
    side = dense.shape[1] // blocks
    for d in range(reps):
        place_vector[d] = tiles[d][pl.ds(slots * part, PAD), :].astype(jnp.int32)
    copy = pltpu.make_async_copy(place_vector, place, sem)
    copy.start()
    dense[...] = jnp.zeros_like(dense)
    copy.wait()
    for d in range(reps):
        for s in range(slots):
            lane = pl.ds(pl.multiple_of(place[d, 0, s] * side, LANES), side)
            at = pl.ds(pl.multiple_of(place[d, 1, s] * part, 8), part)
            dense[at, lane] = dense[at, lane] + tiles[d][pl.ds(s * part, part), :]
    for k in range(dense.shape[0] // side):
        at = pl.ds(k * side, side)
        high, low = halves(dense[at, :])
        high_out[at, :] = high.astype(BF16)
        low_out[at, :] = low.astype(BF16)


def forward_kernel(loops, here, high, low, *refs):
    feats = refs[:loops]
    send, keep, left, acc = refs[loops:]
    rows, width = feats[0].shape
    for k in range(loops):
        at = pl.ds(k * rows, rows)
        upper, lower = halves(feats[k][...].T)
        left[:width, at] = upper.astype(BF16)
        left[width:, at] = lower.astype(BF16)
    both = jnp.dot(left[...], high[...], preferred_element_type=F32)
    rest = jnp.dot(left[:width, :], low[...], preferred_element_type=F32)
    acc[...] = both[:width, :] + both[width:, :] + rest
    half = acc.shape[0] // 2
    core = here[0] & 1
    keep[...] = acc[pl.ds(pl.multiple_of(core * half, 8), half), :]
    send[...] = acc[pl.ds(pl.multiple_of((1 - core) * half, 8), half), :]


def times(high, low, right, width):
    both = jnp.dot(high, right, preferred_element_type=F32)
    rest = jnp.dot(low, right[:, :width], preferred_element_type=F32)
    return both[:, :width] + both[:, width:] + rest


def backward_kernel(
    reps, blocks, groups, here, high, low, mine, other, weight, bias, cotangent, *refs
):
    outs = refs[: len(groups)]
    output, grads, piece_t, agg, right = refs[len(groups) :]
    width, total = agg.shape
    half, side = width // 2, total // blocks
    core = here[0] & 1
    agg[pl.ds(pl.multiple_of(core * half, 8), half), :] = mine[...]
    agg[pl.ds(pl.multiple_of((1 - core) * half, 8), half), :] = other[...]
    piece = width // reps
    piece_t[...] = agg[pl.ds(pl.multiple_of(here[0] * piece, 8), piece), :]
    w = weight[...]
    for b in range(blocks):
        at = pl.ds(b * side, side)
        pre = dot3(agg[:, at].T, w) + bias[...]
        gate = jax.nn.sigmoid(pre)
        output[at, :] = pre * gate
        gradient = cotangent[at, :] * gate * (1.0 + pre * (1.0 - gate))
        grads[at, :] = gradient
        spread = dot3(gradient, w, (((1,), (1,)), ((), ())))
        upper, lower = halves(spread)
        right[at, :width] = upper.astype(BF16)
        right[at, width:] = lower.astype(BF16)
    for group, out in zip(groups, outs):
        size = out.shape[0] // len(group)
        for n, k in enumerate(group):
            at = pl.ds(k * size, size)
            out[pl.ds(n * size, size), :] = times(high[at, :], low[at, :], right[...], width)


def weight_kernel(piece_t, grads, out):
    piece, groups = piece_t.shape[0], grads.shape[1] // LANES
    g = grads[...]
    grad_weight = dot3(piece_t[...], g)
    grad_bias = jnp.sum(g, axis=0, keepdims=True)
    for q in range(groups):
        out[pl.ds(q * piece, piece), :] = grad_weight[:, q * LANES : (q + 1) * LANES]
    tail = [grad_bias[:, q * LANES : (q + 1) * LANES] for q in range(groups)]
    tail.append(jnp.zeros((PAD - groups, LANES), F32))
    out[pl.ds(groups * piece, PAD), :] = jnp.concatenate(tail, axis=0)


def add_kernel(cuts, count, *refs):
    mine, theirs, outs = refs[:count], refs[count : 2 * count], refs[2 * count :]
    for cut, out in zip(cuts, outs):
        to = 0
        for pair, first, rows in cut:
            at = pl.ds(first, rows)
            out[pl.ds(to, rows), :] = mine[pair][at, :] + theirs[pair][at, :]
            to += rows


def add(mine, theirs, cuts=None):
    cuts = cuts or [[(n, 0, x.shape[0])] for n, x in enumerate(mine)]
    total = sum(x.size for x in mine)
    return call(
        functools.partial(add_kernel, cuts, len(mine)),
        [(sum(rows for _, _, rows in cut), mine[0].shape[1]) for cut in cuts],
        [VMEM] * (2 * len(mine)),
        [],
        total,
        12 * total,
        "add",
    )(*mine, *theirs)


def final_kernel(reps, blocks, part, piece, here, *refs):
    parts = refs[:reps]
    grad_features, grad_weight, grad_bias = refs[reps:]
    side = grad_features.shape[0] // blocks
    groups = grad_weight.shape[1] // LANES
    base = blocks * part
    for d in range(reps):
        q = here[0] ^ d
        for b in range(blocks):
            at = pl.ds(pl.multiple_of(b * side + q * part, 8), part)
            grad_features[at, :] = parts[d][pl.ds(b * part, part), :]
        at = pl.ds(pl.multiple_of(q * piece, 8), piece)
        for g in range(groups):
            grad_weight[at, pl.ds(g * LANES, LANES)] = parts[d][pl.ds(base + g * piece, piece), :]
    for g in range(groups):
        row = parts[0][pl.ds(base + groups * piece + g, 1), :]
        grad_bias[:, pl.ds(g * LANES, LANES)] = row


def per_device(features, weight, bias, tile_values, tile_rows, tile_cols, tile_count, cotangent):
    loops, reps = lax.axis_size("loop"), lax.axis_size("rep")
    slots, side = tile_values.shape[0], tile_values.shape[1]
    total, width = features.shape
    wide = weight.shape[1]
    blocks = total // side
    part, piece = side // reps, width // reps
    size, depth = blocks * part, loops * blocks * part
    extra = wide // LANES * piece + PAD
    here = lax.axis_index("rep").astype(jnp.int32).reshape(1)
    loop_at = lax.axis_index("loop").astype(jnp.int32).reshape(1)
    bias = bias.reshape(1, wide)

    def swap(x, axis, bit):
        n = lax.axis_size(axis)
        return lax.ppermute(x, axis, [(i, i ^ bit) for i in range(n)])

    chunks = 4 if slots % 4 == 0 else 1
    sources = (features, tile_values, tile_rows[None], tile_cols[None])
    own, *parcels = call(
        functools.partial(pack_kernel, reps, blocks, part),
        [(size, width)] + [(slots * part + PAD, side)] * reps,
        [SMEM] * 3 + [HBM] * 4,
        [
            pltpu.VMEM((slots, side, side), F32),
            pltpu.VMEM((slots, side, side), F32),
            pltpu.VMEM((1, slots), jnp.int32),
            pltpu.VMEM((1, slots), jnp.int32),
            pltpu.SemaphoreType.DMA((2 + chunks + blocks,)),
        ],
        0,
        2 * tile_values.size * 4,
        "pack",
    )(here, loop_at, tile_count, *[pltpu.with_memory_space_constraint(x, pltpu.HBM) for x in sources])
    tiles = [parcels[0]] + [swap(parcels[d], "rep", d) for d in range(1, reps)]

    feats = {0: own}
    bit = loops // 2
    while bit:
        for k in list(feats):
            feats[k | bit] = swap(feats[k], "loop", bit)
        bit //= 2

    high, low = call(
        functools.partial(build_kernel, reps, blocks, part, slots),
        [((depth, total), BF16)] * 2,
        [VMEM] * (reps + 3),
        [
            pltpu.VMEM((depth, total), F32),
            pltpu.VMEM((reps, PAD, LANES), jnp.int32),
            pltpu.SMEM((reps, PAD, LANES), jnp.int32),
            pltpu.SemaphoreType.DMA,
        ],
        0,
        8 << 20,
        "build",
    )(*tiles, weight, bias, cotangent)

    send, keep = call(
        functools.partial(forward_kernel, loops),
        [(width // 2, total)] * 2,
        [SMEM] + [VMEM] * (2 + loops),
        [pltpu.VMEM((2 * width, depth), BF16), pltpu.VMEM((width, total), F32)],
        2 * depth * total * width * 3,
        4 << 20,
        "forward",
    )(here, high, low, *[feats[k] for k in range(loops)])
    (mine,) = add([keep], [swap(send, "rep", 1)])
    bit = 2
    while bit < reps:
        (mine,) = add([mine], [swap(mine, "rep", bit)])
        bit *= 2
    other = swap(mine, "rep", 1)

    even = range(0, loops, 2)
    on, stay = [k for k in even if k & 2], [k for k in even if not k & 2]
    groups = [[k | 1 for k in on], [k | 1 for k in stay], on, stay]
    *moved, output, grads, piece_t = call(
        functools.partial(backward_kernel, reps, blocks, groups),
        [(len(g) * size, width) for g in groups] + [(total, wide)] * 2 + [(piece, total)],
        [SMEM] + [VMEM] * 7,
        [pltpu.VMEM((width, total), F32), pltpu.VMEM((total, 2 * width), BF16)],
        2 * depth * total * width * 3,
        4 << 20,
        "backward",
    )(here, high, low, mine, other, weight, bias, cotangent)
    on_term, stay_term = swap(moved[0], "loop", 1), swap(moved[1], "loop", 1)
    (grad,) = call(
        weight_kernel,
        [(extra, LANES)],
        [VMEM] * 2,
        [],
        2 * piece * total * wide * 3,
        1 << 20,
        "weight",
    )(piece_t, grads)

    last = loops // 2
    grad_term = swap(grad, "loop", last)
    going, grad = add([moved[2], grad], [on_term, grad_term])
    term = swap(going, "loop", 2)
    grad_term = swap(grad, "loop", 1)
    (held,) = add([moved[3]], [stay_term])
    bit, rest = 2, stay
    while bit < last:
        ahead = [(0, n * size, size) for n, k in enumerate(rest) if k & (2 * bit)]
        behind = [(0, n * size, size) for n, k in enumerate(rest) if not k & (2 * bit)]
        rest = [k for k in rest if not k & (2 * bit)]
        going, held, grad = add([held, grad], [term, grad_term], [ahead, behind, [(1, 0, extra)]])
        term = swap(going, "loop", 2 * bit)
        grad_term = swap(grad, "loop", bit)
        bit *= 2
    (both,) = add([held, grad], [term, grad_term], [[(0, 0, size), (1, 0, extra)]])

    parts = {0: both}
    bit = reps // 2
    while bit:
        for k in list(parts):
            parts[k | bit] = swap(parts[k], "rep", bit)
        bit //= 2
    grad_features, grad_weight, grad_bias = call(
        functools.partial(final_kernel, reps, blocks, part, piece),
        [(total, width), (width, wide), (1, wide)],
        [SMEM] + [VMEM] * reps,
        [],
        0,
        2 * total * width * 4,
        "final",
    )(here, *[parts[d] for d in range(reps)])
    return (output, grad_features, grad_weight, grad_bias.reshape(wide))


def solution(mesh):
    return jax.shard_map(
        per_device,
        mesh=mesh,
        in_specs=(
            P("loop", None),
            P(),
            P(),
            P(("loop", "rep"), None, None),
            P(("loop", "rep")),
            P(("loop", "rep")),
            P(("loop", "rep")),
            P("loop", None),
        ),
        out_specs=(P("loop", None), P("loop", None), P(), P()),
        check_vma=False,
    )
```

```python
import functools

import jax
import jax.numpy as jnp
from jax import lax
from jax.experimental import pallas as pl
from jax.experimental.pallas import tpu as pltpu
from jax.sharding import PartitionSpec as P


LANES = 128
PAD = 8
F32 = jnp.float32
BF16 = jnp.bfloat16
VMEM = pl.BlockSpec(memory_space=pltpu.VMEM)
SMEM = pl.BlockSpec(memory_space=pltpu.SMEM)
HBM = pl.BlockSpec(memory_space=pltpu.HBM)


def halves(x):
    high = x.astype(BF16).astype(F32)
    return high, x - high


def dot3(a, b, dims=(((1,), (0,)), ((), ()))):
    ah, al = halves(a)
    bh, bl = halves(b)
    ah, al, bh, bl = (v.astype(BF16) for v in (ah, al, bh, bl))
    dot = functools.partial(lax.dot_general, dimension_numbers=dims, preferred_element_type=F32)
    return dot(ah, bh) + dot(ah, bl) + dot(al, bh)


def call(kernel, out_shapes, in_specs, scratch, flops, moved, limit=24, aliases=None):
    return pl.pallas_call(
        kernel,
        input_output_aliases=aliases or {},
        out_shape=[
            jax.ShapeDtypeStruct(*(s if isinstance(s[0], tuple) else (s, F32))) for s in out_shapes
        ],
        in_specs=in_specs,
        out_specs=[VMEM] * len(out_shapes),
        scratch_shapes=scratch,
        compiler_params=pltpu.CompilerParams(vmem_limit_bytes=limit << 20),
        cost_estimate=pl.CostEstimate(flops=flops, bytes_accessed=moved, transcendentals=0),
    )


def join_kernel(*refs):
    at = 0
    for ref in refs[:-1]:
        refs[-1][pl.ds(at, ref.shape[0]), :] = ref[...]
        at += ref.shape[0]


def pack_kernel(reps, loops, blocks, part, rep_at, at_loop, count, features, tiles, rows, cols, *refs):
    own, outs = refs[0], refs[1 : 1 + reps]
    held, turned, row_ids, col_ids, sem = refs[1 + reps :]
    here, loop_at = rep_at[0], at_loop[0]
    slots, side = tiles.shape[0], tiles.shape[1]
    chunks = sem.shape[0] - 2 - blocks
    step = slots // chunks
    small = [
        pltpu.make_async_copy(source, target, sem.at[n])
        for n, (source, target) in enumerate([(rows, row_ids), (cols, col_ids)])
    ]
    large = [
        pltpu.make_async_copy(
            tiles.at[pl.ds(n * step, step)], held.at[pl.ds(n * step, step)], sem.at[2 + n]
        )
        for n in range(chunks)
    ]
    pieces = [
        pltpu.make_async_copy(
            features.at[pl.ds(pl.multiple_of(b * side + here * part, 8), part), :],
            own.at[pl.ds(b * part, part), :],
            sem.at[2 + chunks + b],
        )
        for b in range(blocks)
    ]
    for copy in small + large + pieces:
        copy.start()
    for copy in small:
        copy.wait()
    local_rows = row_ids[...] - loop_at * blocks
    shift = blocks.bit_length() - 1
    away = (col_ids[...] >> shift) ^ loop_at
    low = min(loops, 4) - 1
    other_way = (away & ~low) | ((away & low) >> 1) | jnp.where(away & 1 == 1, (low + 1) // 2, 0)
    for d in range(reps):
        second = ((here ^ d) & 1) * jnp.ones_like(away)
        order = jnp.where(second == 1, away, other_way)
        column = (order << shift) | (col_ids[...] & (blocks - 1))
        meta = jnp.concatenate([local_rows, column], axis=0).astype(F32)
        outs[d][pl.ds(slots * part, 2), pl.ds(0, slots)] = meta
    alive = count[0]
    for n in range(chunks):
        large[n].wait()
        for s in range(n * step, (n + 1) * step):
            turned[s] = jnp.where(s < alive, held[s].T, jnp.zeros((side, side), F32))
            for d in range(reps):
                start = pl.multiple_of((here ^ d) * part, 8)
                outs[d][pl.ds(s * part, part), :] = turned[s, pl.ds(start, part), :]
    for copy in pieces:
        copy.wait()


def place_parts(blocks, part, slots, tiles, dense, place_vector, place, sem, clear):
    side = dense.shape[1] // blocks
    for d, tile in enumerate(tiles):
        place_vector[d] = tile[pl.ds(slots * part, PAD), :].astype(jnp.int32)
    copy = pltpu.make_async_copy(place_vector, place, sem)
    copy.start()
    if clear:
        dense[...] = jnp.zeros_like(dense)
    copy.wait()
    for d, tile in enumerate(tiles):
        for s in range(slots):
            lane = pl.ds(pl.multiple_of(place[d, 0, s] * side, LANES), side)
            at = pl.ds(pl.multiple_of(place[d, 1, s] * part, 8), part)
            dense[at, lane] = dense[at, lane] + tile[pl.ds(s * part, part), :]


def near_kernel(blocks, part, slots, *refs):
    place_parts(blocks, part, slots, refs[:-4], refs[-4], *refs[-3:], True)


def far_kernel(blocks, part, slots, count, *refs):
    tiles = refs[1 : 1 + count]
    dense, high_out, low_out = refs[-6:-3]
    place_parts(blocks, part, slots, tiles, dense, *refs[-3:], False)
    side = dense.shape[1] // blocks
    for k in range(dense.shape[0] // side):
        at = pl.ds(k * side, side)
        high, low = halves(dense[at, :])
        high_out[at, :] = high.astype(BF16)
        low_out[at, :] = low.astype(BF16)


def forward_kernel(orders, here, high, low, *refs):
    feats = refs[: len(orders)]
    send, keep, left, acc = refs[len(orders) :]
    width = left.shape[0] // 2
    for order, feat in zip(orders, feats):
        rows = feat.shape[0] // len(order)
        for n, k in enumerate(order):
            at = pl.ds(k * rows, rows)
            upper, lower = halves(feat[pl.ds(n * rows, rows), :].T)
            left[:width, at] = upper.astype(BF16)
            left[width:, at] = lower.astype(BF16)
    both = jnp.dot(left[...], high[...], preferred_element_type=F32)
    rest = jnp.dot(left[:width, :], low[...], preferred_element_type=F32)
    acc[...] = both[:width, :] + both[width:, :] + rest
    half = acc.shape[0] // 2
    core = here[0] & 1
    keep[...] = acc[pl.ds(pl.multiple_of(core * half, 8), half), :]
    send[...] = acc[pl.ds(pl.multiple_of((1 - core) * half, 8), half), :]


def times(high, low, right, width):
    both = jnp.dot(high, right, preferred_element_type=F32)
    rest = jnp.dot(low, right[:, :width], preferred_element_type=F32)
    return both[:, :width] + both[:, width:] + rest


def products(group, size, high, low, right, out):
    for n, k in enumerate(group):
        at = pl.ds(k * size, size)
        value = times(high[at, :], low[at, :], right[...], right.shape[1] // 2)
        out[pl.ds(n * size, size), :] = value


def dense_kernel(
    blocks, group, size, here, high, low, mine, other, weight, bias, cotangent, *refs
):
    out, output, grads, piece_t, right, agg = refs
    width, total = agg.shape
    half, side = width // 2, total // blocks
    core = here[0] & 1
    agg[pl.ds(pl.multiple_of(core * half, 8), half), :] = mine[...]
    agg[pl.ds(pl.multiple_of((1 - core) * half, 8), half), :] = other[...]
    w = weight[...]
    for b in range(blocks):
        at = pl.ds(b * side, side)
        pre = dot3(agg[:, at].T, w) + bias[...]
        gate = jax.nn.sigmoid(pre)
        output[at, :] = pre * gate
        gradient = cotangent[at, :] * gate * (1.0 + pre * (1.0 - gate))
        grads[at, :] = gradient
        spread = dot3(gradient, w, (((1,), (1,)), ((), ())))
        upper, lower = halves(spread)
        right[at, :width] = upper.astype(BF16)
        right[at, width:] = lower.astype(BF16)
    products(group, size, high, low, right, out)
    piece = piece_t.shape[0]
    piece_t[...] = agg[pl.ds(pl.multiple_of(here[0] * piece, 8), piece), :]


def rest_kernel(groups, size, high, low, right, *outs):
    for group, out in zip(groups, outs):
        products(group, size, high, low, right, out)


def weight_kernel(piece_t, grads, out):
    piece, parts = piece_t.shape[0], grads.shape[1] // LANES
    g = grads[...]
    grad_weight = dot3(piece_t[...], g)
    grad_bias = jnp.sum(g, axis=0, keepdims=True)
    for q in range(parts):
        out[pl.ds(q * piece, piece), :] = grad_weight[:, q * LANES : (q + 1) * LANES]
    tail = [grad_bias[:, q * LANES : (q + 1) * LANES] for q in range(parts)]
    tail.append(jnp.zeros((PAD - parts, LANES), F32))
    out[pl.ds(parts * piece, PAD), :] = jnp.concatenate(tail, axis=0)


def add_kernel(cuts, count, *refs):
    mine, theirs, outs = refs[:count], refs[count : 2 * count], refs[2 * count :]
    for cut, out in zip(cuts, outs):
        to = 0
        for pair, first, second, rows in cut:
            left, right = pl.ds(first, rows), pl.ds(second, rows)
            out[pl.ds(to, rows), :] = mine[pair][left, :] + theirs[pair][right, :]
            to += rows


def add(mine, theirs, cuts=None):
    cuts = cuts or [[(n, 0, 0, x.shape[0])] for n, x in enumerate(mine)]
    total = sum(x.size for x in mine)
    return call(
        functools.partial(add_kernel, cuts, len(mine)),
        [(sum(cut[-1] for cut in cuts_of), mine[0].shape[1]) for cuts_of in cuts],
        [VMEM] * (2 * len(mine)),
        [],
        total,
        12 * total,
    )(*mine, *theirs)


def final_kernel(reps, blocks, part, piece, here, *refs):
    parts = refs[:reps]
    grad_features, grad_weight, grad_bias = refs[reps:]
    side = grad_features.shape[0] // blocks
    groups = grad_weight.shape[1] // LANES
    base = blocks * part
    for d in range(reps):
        q = here[0] ^ d
        for b in range(blocks):
            at = pl.ds(pl.multiple_of(b * side + q * part, 8), part)
            grad_features[at, :] = parts[d][pl.ds(b * part, part), :]
        at = pl.ds(pl.multiple_of(q * piece, 8), piece)
        for g in range(groups):
            grad_weight[at, pl.ds(g * LANES, LANES)] = parts[d][pl.ds(base + g * piece, piece), :]
    for g in range(groups):
        row = parts[0][pl.ds(base + groups * piece + g, 1), :]
        grad_bias[:, pl.ds(g * LANES, LANES)] = row


def per_device(features, weight, bias, tile_values, tile_rows, tile_cols, tile_count, cotangent):
    loops, reps = lax.axis_size("loop"), lax.axis_size("rep")
    slots, side = tile_values.shape[0], tile_values.shape[1]
    total, width = features.shape
    wide = weight.shape[1]
    blocks = total // side
    part, piece = side // reps, width // reps
    size, depth = blocks * part, loops * blocks * part
    extra = wide // LANES * piece + PAD
    here = lax.axis_index("rep").astype(jnp.int32).reshape(1)
    loop_at = lax.axis_index("loop").astype(jnp.int32).reshape(1)
    bias = bias.reshape(1, wide)

    def swap(x, axis, bit):
        pairs, low = [], min(loops, 4)
        for a in range(loops):
            for b in range(reps):
                turn = axis == "loop" and bit < low and not b & 1
                over = (2 * bit if 2 * bit < low else 1) if turn else bit
                to = (a ^ over, b) if axis == "loop" else (a, b ^ bit)
                pairs.append((a * reps + b, to[0] * reps + to[1]))
        return lax.ppermute(x, ("loop", "rep"), pairs)

    def join(*arrays):
        shape = (sum(x.shape[0] for x in arrays), arrays[0].shape[1])
        return call(
            join_kernel, [shape], [VMEM] * len(arrays), [], 0, 8 * shape[0] * shape[1]
        )(*arrays)[0]

    chunks = 4 if slots % 4 == 0 else 1
    sources = (features, tile_values, tile_rows[None], tile_cols[None])
    own, *parcels = call(
        functools.partial(pack_kernel, reps, loops, blocks, part),
        [(size, width)] + [(slots * part + PAD, side)] * reps,
        [SMEM] * 3 + [HBM] * 4,
        [
            pltpu.VMEM((slots, side, side), F32),
            pltpu.VMEM((slots, side, side), F32),
            pltpu.VMEM((1, slots), jnp.int32),
            pltpu.VMEM((1, slots), jnp.int32),
            pltpu.SemaphoreType.DMA((2 + chunks + blocks,)),
        ],
        0,
        2 * tile_values.size * 4,
    )(here, loop_at, tile_count, *[pltpu.with_memory_space_constraint(x, pltpu.HBM) for x in sources])
    tiles = [parcels[0]] + [swap(parcels[d], "rep", d) for d in range(1, reps)]

    bit = loops // 2
    feats, orders = [own, swap(own, "loop", bit)], [[0], [bit]]
    bit //= 2
    while bit > 1:
        feats, order = [join(*feats)], sum(orders, [])
        feats.append(swap(feats[0], "loop", bit))
        orders = [order, [k | bit for k in order]]
        bit //= 2
    feats += [swap(x, "loop", 1) for x in feats]
    orders += [[k | 1 for k in order] for order in orders]

    def scratch(count):
        return [
            pltpu.VMEM((count, PAD, LANES), jnp.int32),
            pltpu.SMEM((count, PAD, LANES), jnp.int32),
            pltpu.SemaphoreType.DMA,
        ]

    (dense,) = call(
        functools.partial(near_kernel, blocks, part, slots),
        [(depth, total)],
        [VMEM] * 2,
        scratch(2),
        0,
        4 << 20,
    )(*tiles[:2])
    _, high, low = call(
        functools.partial(far_kernel, blocks, part, slots, reps - 2),
        [(depth, total)] + [((depth, total), BF16)] * 2,
        [VMEM] * (reps + 2),
        scratch(reps - 2),
        0,
        8 << 20,
        aliases={0: 0},
    )(dense, *tiles[2:], weight, bias, cotangent)

    send, keep = call(
        functools.partial(forward_kernel, orders),
        [(width // 2, total)] * 2,
        [SMEM] + [VMEM] * (2 + len(feats)),
        [pltpu.VMEM((2 * width, depth), BF16), pltpu.VMEM((width, total), F32)],
        2 * depth * total * width * 3,
        4 << 20,
    )(here, high, low, *feats)
    (mine,) = add([keep], [swap(send, "rep", 1)])
    bit = 2
    while bit < reps:
        (mine,) = add([mine], [swap(mine, "rep", bit)])
        bit *= 2
    other = swap(mine, "rep", 1)

    even = range(0, loops, 2)
    on, stay = [k for k in even if k & 2], [k for k in even if not k & 2]
    groups = [[k | 1 for k in on], [k | 1 for k in stay], on, stay]
    first, output, grads, piece_t, right = call(
        functools.partial(dense_kernel, blocks, groups[0], size),
        [(len(on) * size, width)]
        + [(total, wide)] * 2
        + [(piece, total), ((total, 2 * width), BF16)],
        [SMEM] + [VMEM] * 7,
        [pltpu.VMEM((width, total), F32)],
        2 * depth * total * width,
        4 << 20,
    )(here, high, low, mine, other, weight, bias, cotangent)
    on_term = swap(first, "loop", 1)
    sent, on_own, stay_own = call(
        functools.partial(rest_kernel, groups[1:], size),
        [(len(g) * size, width) for g in groups[1:]],
        [VMEM] * 3,
        [],
        2 * depth * total * width * 2,
        3 << 20,
    )(high, low, right)
    stay_term = swap(sent, "loop", 1)
    (grad,) = call(
        weight_kernel, [(extra, LANES)], [VMEM] * 2, [], 2 * piece * total * wide * 3, 1 << 20
    )(piece_t, grads)

    grad_term = swap(grad, "loop", loops // 2)
    (going,) = add([on_own], [on_term])
    term = swap(going, "loop", 2)
    (grad,) = add([grad], [grad_term])
    grad_term = swap(grad, "loop", 1)
    (held,) = add([stay_own], [stay_term])
    bit, rest = 2, stay
    while bit < loops // 2:
        ahead = [(0, n * size, n * size, size) for n, k in enumerate(rest) if k & (2 * bit)]
        behind = [(0, n * size, n * size, size) for n, k in enumerate(rest) if not k & (2 * bit)]
        rest = [k for k in rest if not k & (2 * bit)]
        going, held = add([held], [term], [ahead, behind])
        term = swap(going, "loop", 2 * bit)
        (grad,) = add([grad], [grad_term])
        grad_term = swap(grad, "loop", bit)
        bit *= 2
    (both,) = add([held, grad], [term, grad_term], [[(0, 0, 0, size), (1, 0, 0, extra)]])

    parts = {0: both}
    bit = reps // 2
    while bit:
        for k in list(parts):
            parts[k | bit] = swap(parts[k], "rep", bit)
        bit //= 2
    output = join(output)
    grad_features, grad_weight, grad_bias = call(
        functools.partial(final_kernel, reps, blocks, part, piece),
        [(total, width), (width, wide), (1, wide)],
        [SMEM] + [VMEM] * reps,
        [],
        0,
        2 * total * width * 4,
    )(here, *[parts[d] for d in range(reps)])
    return (output, grad_features, grad_weight, grad_bias.reshape(wide))


def solution(mesh):
    return jax.shard_map(
        per_device,
        mesh=mesh,
        in_specs=(
            P("loop", None),
            P(),
            P(),
            P(("loop", "rep"), None, None),
            P(("loop", "rep")),
            P(("loop", "rep")),
            P(("loop", "rep")),
            P("loop", None),
        ),
        out_specs=(P("loop", None), P("loop", None), P(), P()),
        check_vma=False,
    )
```

```python
import functools

import jax
import jax.numpy as jnp
from jax import lax
from jax.experimental import pallas as pl
from jax.experimental.pallas import tpu as pltpu
from jax.sharding import PartitionSpec as P


LANES = 128
PAD = 8
F32 = jnp.float32
BF16 = jnp.bfloat16
VMEM = pl.BlockSpec(memory_space=pltpu.VMEM)
SMEM = pl.BlockSpec(memory_space=pltpu.SMEM)
HBM = pl.BlockSpec(memory_space=pltpu.HBM)


def halves(x):
    high = x.astype(BF16).astype(F32)
    return high, x - high


def dot3(a, b, dims=(((1,), (0,)), ((), ()))):
    ah, al = halves(a)
    bh, bl = halves(b)
    ah, al, bh, bl = (v.astype(BF16) for v in (ah, al, bh, bl))
    dot = functools.partial(lax.dot_general, dimension_numbers=dims, preferred_element_type=F32)
    return dot(ah, bh) + dot(ah, bl) + dot(al, bh)


def call(kernel, out_shapes, in_specs, scratch, flops, moved, limit=24, aliases=None):
    return pl.pallas_call(
        kernel,
        input_output_aliases=aliases or {},
        out_shape=[
            jax.ShapeDtypeStruct(*(s if isinstance(s[0], tuple) else (s, F32))) for s in out_shapes
        ],
        in_specs=in_specs,
        out_specs=[VMEM] * len(out_shapes),
        scratch_shapes=scratch,
        compiler_params=pltpu.CompilerParams(vmem_limit_bytes=limit << 20),
        cost_estimate=pl.CostEstimate(flops=flops, bytes_accessed=moved, transcendentals=0),
    )


def join_kernel(*refs):
    at = 0
    for ref in refs[:-1]:
        refs[-1][pl.ds(at, ref.shape[0]), :] = ref[...]
        at += ref.shape[0]


def pack_kernel(reps, loops, blocks, part, rep_at, at_loop, count, features, tiles, rows, cols, *refs):
    own, outs = refs[0], refs[1 : 1 + reps]
    held, turned, row_ids, col_ids, sem = refs[1 + reps :]
    here, loop_at = rep_at[0], at_loop[0]
    slots, side = tiles.shape[0], tiles.shape[1]
    chunks = sem.shape[0] - 2 - blocks
    step = slots // chunks
    small = [
        pltpu.make_async_copy(source, target, sem.at[n])
        for n, (source, target) in enumerate([(rows, row_ids), (cols, col_ids)])
    ]
    large = [
        pltpu.make_async_copy(
            tiles.at[pl.ds(n * step, step)], held.at[pl.ds(n * step, step)], sem.at[2 + n]
        )
        for n in range(chunks)
    ]
    pieces = [
        pltpu.make_async_copy(
            features.at[pl.ds(pl.multiple_of(b * side + here * part, 8), part), :],
            own.at[pl.ds(b * part, part), :],
            sem.at[2 + chunks + b],
        )
        for b in range(blocks)
    ]
    for copy in small + large + pieces:
        copy.start()
    for copy in small:
        copy.wait()
    local_rows = row_ids[...] - loop_at * blocks
    shift = blocks.bit_length() - 1
    away = (col_ids[...] >> shift) ^ loop_at
    low = min(loops, 4) - 1
    other_way = (away & ~low) | ((away & low) >> 1) | jnp.where(away & 1 == 1, (low + 1) // 2, 0)
    for d in range(reps):
        second = ((here ^ d) & 1) * jnp.ones_like(away)
        order = jnp.where(second == 1, away, other_way)
        column = (order << shift) | (col_ids[...] & (blocks - 1))
        meta = jnp.concatenate([local_rows, column], axis=0).astype(F32)
        outs[d][pl.ds(slots * part, 2), pl.ds(0, slots)] = meta
    alive = count[0]
    for n in range(chunks):
        large[n].wait()
        for s in range(n * step, (n + 1) * step):
            turned[s] = jnp.where(s < alive, held[s].T, jnp.zeros((side, side), F32))
            for d in range(reps):
                start = pl.multiple_of((here ^ d) * part, 8)
                outs[d][pl.ds(s * part, part), :] = turned[s, pl.ds(start, part), :]
    for copy in pieces:
        copy.wait()


def place_parts(blocks, part, slots, tiles, dense, place_vector, place, sem, clear, both=()):
    side = dense.shape[1] // blocks
    for d, tile in enumerate(tiles):
        place_vector[d] = tile[pl.ds(slots * part, PAD), :].astype(jnp.int32)
    copy = pltpu.make_async_copy(place_vector, place, sem)
    copy.start()
    if clear:
        dense[...] = jnp.zeros_like(dense)
    copy.wait()
    for d, tile in enumerate(tiles):
        for s in range(slots):
            lane = pl.ds(pl.multiple_of(place[d, 0, s] * side, LANES), side)
            at = pl.ds(pl.multiple_of(place[d, 1, s] * part, part), part)
            value = dense[at, lane] + tile[pl.ds(s * part, part), :]
            dense[at, lane] = value
            for ref, term in zip(both, halves(value)):
                ref[at, lane] = term.astype(BF16)


def split(dense, high_out, low_out):
    side = 8 * 16
    for k in range(dense.shape[0] // side):
        at = pl.ds(k * side, side)
        high, low = halves(dense[at, :])
        high_out[at, :] = high.astype(BF16)
        low_out[at, :] = low.astype(BF16)


def near_kernel(blocks, part, slots, *refs):
    dense, high_out, low_out = refs[-6:-3]
    place_parts(blocks, part, slots, refs[:-6], dense, *refs[-3:], True)
    split(dense, high_out, low_out)


def far_kernel(blocks, part, slots, count, *refs):
    tiles = refs[3 : 3 + count]
    dense, high_out, low_out = refs[-6:-3]
    both = (high_out, low_out) if part % 16 == 0 else ()
    place_parts(blocks, part, slots, tiles, dense, *refs[-3:], False, both)
    if not both:
        split(dense, high_out, low_out)


def forward_kernel(orders, here, high, low, *refs):
    feats = refs[: len(orders)]
    send, keep, left, acc = refs[len(orders) :]
    width = left.shape[0] // 2
    for order, feat in zip(orders, feats):
        rows = feat.shape[0] // len(order)
        for n, k in enumerate(order):
            at = pl.ds(k * rows, rows)
            upper, lower = halves(feat[pl.ds(n * rows, rows), :].T)
            left[:width, at] = upper.astype(BF16)
            left[width:, at] = lower.astype(BF16)
    both = jnp.dot(left[...], high[...], preferred_element_type=F32)
    rest = jnp.dot(left[:width, :], low[...], preferred_element_type=F32)
    acc[...] = both[:width, :] + both[width:, :] + rest
    half = acc.shape[0] // 2
    core = here[0] & 1
    keep[...] = acc[pl.ds(pl.multiple_of(core * half, 8), half), :]
    send[...] = acc[pl.ds(pl.multiple_of((1 - core) * half, 8), half), :]


def times(high, low, right, width):
    both = jnp.dot(high, right, preferred_element_type=F32)
    rest = jnp.dot(low, right[:, :width], preferred_element_type=F32)
    return both[:, :width] + both[:, width:] + rest


def products(group, size, high, low, right, out):
    for n, k in enumerate(group):
        at = pl.ds(k * size, size)
        value = times(high[at, :], low[at, :], right[...], right.shape[1] // 2)
        out[pl.ds(n * size, size), :] = value


def dense_kernel(
    blocks, group, size, here, high, low, mine, other, weight, bias, cotangent, *refs
):
    out, output, grads, piece_t, right, agg = refs
    width, total = agg.shape
    half, side = width // 2, total // blocks
    core = here[0] & 1
    agg[pl.ds(pl.multiple_of(core * half, 8), half), :] = mine[...]
    agg[pl.ds(pl.multiple_of((1 - core) * half, 8), half), :] = other[...]
    w = weight[...]
    for b in range(blocks):
        at = pl.ds(b * side, side)
        pre = dot3(agg[:, at].T, w) + bias[...]
        gate = jax.nn.sigmoid(pre)
        output[at, :] = pre * gate
        gradient = cotangent[at, :] * gate * (1.0 + pre * (1.0 - gate))
        grads[at, :] = gradient
        spread = dot3(gradient, w, (((1,), (1,)), ((), ())))
        upper, lower = halves(spread)
        right[at, :width] = upper.astype(BF16)
        right[at, width:] = lower.astype(BF16)
    products(group, size, high, low, right, out)
    piece = piece_t.shape[0]
    piece_t[...] = agg[pl.ds(pl.multiple_of(here[0] * piece, 8), piece), :]


def rest_kernel(groups, size, high, low, right, *outs):
    for group, out in zip(groups, outs):
        products(group, size, high, low, right, out)


def weight_kernel(piece_t, grads, out):
    piece, parts = piece_t.shape[0], grads.shape[1] // LANES
    g = grads[...]
    grad_weight = dot3(piece_t[...], g)
    grad_bias = jnp.sum(g, axis=0, keepdims=True)
    for q in range(parts):
        out[pl.ds(q * piece, piece), :] = grad_weight[:, q * LANES : (q + 1) * LANES]
    tail = [grad_bias[:, q * LANES : (q + 1) * LANES] for q in range(parts)]
    tail.append(jnp.zeros((PAD - parts, LANES), F32))
    out[pl.ds(parts * piece, PAD), :] = jnp.concatenate(tail, axis=0)


def add_kernel(cuts, count, *refs):
    mine, theirs, outs = refs[:count], refs[count : 2 * count], refs[2 * count :]
    for cut, out in zip(cuts, outs):
        to = 0
        for pair, first, second, rows in cut:
            left, right = pl.ds(first, rows), pl.ds(second, rows)
            out[pl.ds(to, rows), :] = mine[pair][left, :] + theirs[pair][right, :]
            to += rows


def add(mine, theirs, cuts=None):
    cuts = cuts or [[(n, 0, 0, x.shape[0])] for n, x in enumerate(mine)]
    total = sum(x.size for x in mine)
    return call(
        functools.partial(add_kernel, cuts, len(mine)),
        [(sum(cut[-1] for cut in cuts_of), mine[0].shape[1]) for cuts_of in cuts],
        [VMEM] * (2 * len(mine)),
        [],
        total,
        12 * total,
    )(*mine, *theirs)


def final_kernel(reps, blocks, part, piece, here, *refs):
    parts, weights = refs[:reps], refs[reps : 2 * reps]
    grad_features, grad_weight, grad_bias = refs[2 * reps :]
    side = grad_features.shape[0] // blocks
    groups = grad_weight.shape[1] // LANES
    for d in range(reps):
        q = here[0] ^ d
        for b in range(blocks):
            at = pl.ds(pl.multiple_of(b * side + q * part, 8), part)
            grad_features[at, :] = parts[d][pl.ds(b * part, part), :]
        at = pl.ds(pl.multiple_of(q * piece, 8), piece)
        for g in range(groups):
            grad_weight[at, pl.ds(g * LANES, LANES)] = weights[d][pl.ds(g * piece, piece), :]
    for g in range(groups):
        row = weights[0][pl.ds(groups * piece + g, 1), :]
        grad_bias[:, pl.ds(g * LANES, LANES)] = row


def per_device(features, weight, bias, tile_values, tile_rows, tile_cols, tile_count, cotangent):
    loops, reps = lax.axis_size("loop"), lax.axis_size("rep")
    slots, side = tile_values.shape[0], tile_values.shape[1]
    total, width = features.shape
    wide = weight.shape[1]
    blocks = total // side
    part, piece = side // reps, width // reps
    size, depth = blocks * part, loops * blocks * part
    extra = wide // LANES * piece + PAD
    here = lax.axis_index("rep").astype(jnp.int32).reshape(1)
    loop_at = lax.axis_index("loop").astype(jnp.int32).reshape(1)
    bias = bias.reshape(1, wide)

    def swap(x, axis, bit):
        pairs, low = [], min(loops, 4)
        for a in range(loops):
            for b in range(reps):
                turn = axis == "loop" and bit < low and not b & 1
                over = (2 * bit if 2 * bit < low else 1) if turn else bit
                to = (a ^ over, b) if axis == "loop" else (a, b ^ bit)
                pairs.append((a * reps + b, to[0] * reps + to[1]))
        return lax.ppermute(x, ("loop", "rep"), pairs)

    def join(*arrays):
        shape = (sum(x.shape[0] for x in arrays), arrays[0].shape[1])
        return call(
            join_kernel, [shape], [VMEM] * len(arrays), [], 0, 8 * shape[0] * shape[1]
        )(*arrays)[0]

    chunks = 4 if slots % 4 == 0 else 1
    sources = (features, tile_values, tile_rows[None], tile_cols[None])
    own, *parcels = call(
        functools.partial(pack_kernel, reps, loops, blocks, part),
        [(size, width)] + [(slots * part + PAD, side)] * reps,
        [SMEM] * 3 + [HBM] * 4,
        [
            pltpu.VMEM((slots, side, side), F32),
            pltpu.VMEM((slots, side, side), F32),
            pltpu.VMEM((1, slots), jnp.int32),
            pltpu.VMEM((1, slots), jnp.int32),
            pltpu.SemaphoreType.DMA((2 + chunks + blocks,)),
        ],
        0,
        2 * tile_values.size * 4,
    )(here, loop_at, tile_count, *[pltpu.with_memory_space_constraint(x, pltpu.HBM) for x in sources])
    tiles = [parcels[0]] + [swap(parcels[d], "rep", d) for d in range(1, reps)]

    bit = loops // 2
    feats, orders = [own, swap(own, "loop", bit)], [[0], [bit]]
    bit //= 2
    while bit > 1:
        feats, order = [join(*feats)], sum(orders, [])
        feats.append(swap(feats[0], "loop", bit))
        orders = [order, [k | bit for k in order]]
        bit //= 2
    feats += [swap(x, "loop", 1) for x in feats]
    orders += [[k | 1 for k in order] for order in orders]

    def scratch(count):
        return [
            pltpu.VMEM((count, PAD, LANES), jnp.int32),
            pltpu.SMEM((count, PAD, LANES), jnp.int32),
            pltpu.SemaphoreType.DMA,
        ]

    shapes = [(depth, total)] + [((depth, total), BF16)] * 2
    matrix = call(
        functools.partial(near_kernel, blocks, part, slots),
        shapes,
        [VMEM] * 2,
        scratch(2),
        0,
        8 << 20,
    )(*tiles[:2])
    _, high, low = call(
        functools.partial(far_kernel, blocks, part, slots, reps - 2),
        shapes,
        [VMEM] * (reps + 4),
        scratch(reps - 2),
        0,
        8 << 20,
        aliases={0: 0, 1: 1, 2: 2},
    )(*matrix, *tiles[2:], weight, bias, cotangent)

    send, keep = call(
        functools.partial(forward_kernel, orders),
        [(width // 2, total)] * 2,
        [SMEM] + [VMEM] * (2 + len(feats)),
        [pltpu.VMEM((2 * width, depth), BF16), pltpu.VMEM((width, total), F32)],
        2 * depth * total * width * 3,
        4 << 20,
    )(here, high, low, *feats)
    (mine,) = add([keep], [swap(send, "rep", 1)])
    bit = 2
    while bit < reps:
        (mine,) = add([mine], [swap(mine, "rep", bit)])
        bit *= 2
    other = swap(mine, "rep", 1)

    even = range(0, loops, 2)
    on, stay = [k for k in even if k & 2], [k for k in even if not k & 2]
    groups = [[k | 1 for k in on], [k | 1 for k in stay], on, stay]
    first, output, grads, piece_t, right = call(
        functools.partial(dense_kernel, blocks, groups[0], size),
        [(len(on) * size, width)]
        + [(total, wide)] * 2
        + [(piece, total), ((total, 2 * width), BF16)],
        [SMEM] + [VMEM] * 7,
        [pltpu.VMEM((width, total), F32)],
        2 * depth * total * width,
        4 << 20,
    )(here, high, low, mine, other, weight, bias, cotangent)
    on_term = swap(first, "loop", 1)
    sent, on_own, stay_own = call(
        functools.partial(rest_kernel, groups[1:], size),
        [(len(g) * size, width) for g in groups[1:]],
        [VMEM] * 3,
        [],
        2 * depth * total * width * 2,
        3 << 20,
    )(high, low, right)
    stay_term = swap(sent, "loop", 1)
    (grad,) = call(
        weight_kernel, [(extra, LANES)], [VMEM] * 2, [], 2 * piece * total * wide * 3, 1 << 20
    )(piece_t, grads)

    grad_term = swap(grad, "loop", loops // 2)
    (going,) = add([on_own], [on_term])
    term = swap(going, "loop", 2)
    (grad,) = add([grad], [grad_term])
    grad_term = swap(grad, "loop", 2)
    (held,) = add([stay_own], [stay_term])
    bit, rest = 2, stay
    while bit < loops // 2:
        ahead = [(0, n * size, n * size, size) for n, k in enumerate(rest) if k & (2 * bit)]
        behind = [(0, n * size, n * size, size) for n, k in enumerate(rest) if not k & (2 * bit)]
        rest = [k for k in rest if not k & (2 * bit)]
        going, held = add([held], [term], [ahead, behind])
        term = swap(going, "loop", 2 * bit)
        (grad,) = add([grad], [grad_term])
        grad_term = swap(grad, "loop", bit if bit > 2 else 1)
        bit *= 2
    (mine,) = add([held], [term])
    (grad,) = add([grad], [grad_term])

    def spread(own):
        found = {0: own}
        bit = reps // 2
        while bit:
            for k in list(found):
                found[k | bit] = swap(found[k], "rep", bit)
            bit //= 2
        return [found[d] for d in range(reps)]

    parts, weights = spread(mine), spread(grad)
    output = join(output)
    grad_features, grad_weight, grad_bias = call(
        functools.partial(final_kernel, reps, blocks, part, piece),
        [(total, width), (width, wide), (1, wide)],
        [SMEM] + [VMEM] * (2 * reps),
        [],
        0,
        2 * total * width * 4,
    )(here, *parts, *weights)
    return (output, grad_features, grad_weight, grad_bias.reshape(wide))


def solution(mesh):
    return jax.shard_map(
        per_device,
        mesh=mesh,
        in_specs=(
            P("loop", None),
            P(),
            P(),
            P(("loop", "rep"), None, None),
            P(("loop", "rep")),
            P(("loop", "rep")),
            P(("loop", "rep")),
            P("loop", None),
        ),
        out_specs=(P("loop", None), P("loop", None), P(), P()),
        check_vma=False,
    )
```

```python
import functools

import jax
import jax.numpy as jnp
from jax import lax
from jax.experimental import pallas as pl
from jax.experimental.pallas import tpu as pltpu
from jax.sharding import PartitionSpec as P


LANES = 128
PAD = 8
F32 = jnp.float32
BF16 = jnp.bfloat16
VMEM = pl.BlockSpec(memory_space=pltpu.VMEM)
SMEM = pl.BlockSpec(memory_space=pltpu.SMEM)
HBM = pl.BlockSpec(memory_space=pltpu.HBM)


def halves(x):
    high = x.astype(BF16).astype(F32)
    return high, x - high


def dot3(a, b, dims=(((1,), (0,)), ((), ()))):
    ah, al = halves(a)
    bh, bl = halves(b)
    ah, al, bh, bl = (v.astype(BF16) for v in (ah, al, bh, bl))
    dot = functools.partial(lax.dot_general, dimension_numbers=dims, preferred_element_type=F32)
    return dot(ah, bh) + dot(ah, bl) + dot(al, bh)


def call(kernel, out_shapes, in_specs, scratch, flops, moved, limit=24, aliases=None):
    return pl.pallas_call(
        kernel,
        input_output_aliases=aliases or {},
        out_shape=[
            jax.ShapeDtypeStruct(*(s if isinstance(s[0], tuple) else (s, F32))) for s in out_shapes
        ],
        in_specs=in_specs,
        out_specs=[VMEM] * len(out_shapes),
        scratch_shapes=scratch,
        compiler_params=pltpu.CompilerParams(vmem_limit_bytes=limit << 20),
        cost_estimate=pl.CostEstimate(flops=flops, bytes_accessed=moved, transcendentals=0),
    )


def join_kernel(*refs):
    at = 0
    for ref in refs[:-1]:
        refs[-1][pl.ds(at, ref.shape[0]), :] = ref[...]
        at += ref.shape[0]


def pack_kernel(reps, loops, blocks, part, rep_at, at_loop, count, features, tiles, rows, cols, *refs):
    own, outs = refs[0], refs[1 : 1 + reps]
    held, turned, row_ids, col_ids, sem = refs[1 + reps :]
    here, loop_at = rep_at[0], at_loop[0]
    slots, side = tiles.shape[0], tiles.shape[1]
    chunks = sem.shape[0] - 2 - blocks
    step = slots // chunks
    small = [
        pltpu.make_async_copy(source, target, sem.at[n])
        for n, (source, target) in enumerate([(rows, row_ids), (cols, col_ids)])
    ]
    large = [
        pltpu.make_async_copy(
            tiles.at[pl.ds(n * step, step)], held.at[pl.ds(n * step, step)], sem.at[2 + n]
        )
        for n in range(chunks)
    ]
    pieces = [
        pltpu.make_async_copy(
            features.at[pl.ds(pl.multiple_of(b * side + here * part, 8), part), :],
            own.at[pl.ds(b * part, part), :],
            sem.at[2 + chunks + b],
        )
        for b in range(blocks)
    ]
    for copy in small + large + pieces:
        copy.start()
    for copy in small:
        copy.wait()
    local_rows = row_ids[...] - loop_at * blocks
    shift = blocks.bit_length() - 1
    away = (col_ids[...] >> shift) ^ loop_at
    low = min(loops, 4) - 1
    other_way = (away & ~low) | ((away & low) >> 1) | jnp.where(away & 1 == 1, (low + 1) // 2, 0)
    for d in range(reps):
        second = ((here ^ d) & 1) * jnp.ones_like(away)
        order = jnp.where(second == 1, away, other_way)
        column = (order << shift) | (col_ids[...] & (blocks - 1))
        meta = jnp.concatenate([local_rows, column], axis=0).astype(F32)
        outs[d][pl.ds(slots * part, 2), pl.ds(0, slots)] = meta
    alive = count[0]
    for n in range(chunks):
        large[n].wait()
        for s in range(n * step, (n + 1) * step):
            turned[s] = jnp.where(s < alive, held[s].T, jnp.zeros((side, side), F32))
            for d in range(reps):
                start = pl.multiple_of((here ^ d) * part, 8)
                outs[d][pl.ds(s * part, part), :] = turned[s, pl.ds(start, part), :]
    for copy in pieces:
        copy.wait()


def place_parts(blocks, part, slots, tiles, dense, place_vector, place, sem, clear, both=()):
    side = dense.shape[1] // blocks
    for d, tile in enumerate(tiles):
        place_vector[d] = tile[pl.ds(slots * part, PAD), :].astype(jnp.int32)
    copy = pltpu.make_async_copy(place_vector, place, sem)
    copy.start()
    if clear:
        dense[...] = jnp.zeros_like(dense)
    copy.wait()
    for d, tile in enumerate(tiles):
        for s in range(slots):
            lane = pl.ds(pl.multiple_of(place[d, 0, s] * side, LANES), side)
            at = pl.ds(pl.multiple_of(place[d, 1, s] * part, part), part)
            value = dense[at, lane] + tile[pl.ds(s * part, part), :]
            dense[at, lane] = value
            for ref, term in zip(both, halves(value)):
                ref[at, lane] = term.astype(BF16)


def split(dense, high_out, low_out):
    side = 8 * 16
    for k in range(dense.shape[0] // side):
        at = pl.ds(k * side, side)
        high, low = halves(dense[at, :])
        high_out[at, :] = high.astype(BF16)
        low_out[at, :] = low.astype(BF16)


def near_kernel(blocks, part, slots, *refs):
    dense, high_out, low_out = refs[-6:-3]
    place_parts(blocks, part, slots, refs[:-6], dense, *refs[-3:], True)
    split(dense, high_out, low_out)


def far_kernel(blocks, part, slots, count, *refs):
    tiles = refs[3 : 3 + count]
    dense, high_out, low_out = refs[-6:-3]
    both = (high_out, low_out) if part % 16 == 0 else ()
    place_parts(blocks, part, slots, tiles, dense, *refs[-3:], False, both)
    if not both:
        split(dense, high_out, low_out)


def forward_kernel(orders, here, high, low, *refs):
    feats = refs[: len(orders)]
    send, keep, left, acc = refs[len(orders) :]
    width = left.shape[0] // 2
    for order, feat in zip(orders, feats):
        rows = feat.shape[0] // len(order)
        for n, k in enumerate(order):
            at = pl.ds(k * rows, rows)
            upper, lower = halves(feat[pl.ds(n * rows, rows), :].T)
            left[:width, at] = upper.astype(BF16)
            left[width:, at] = lower.astype(BF16)
    both = jnp.dot(left[...], high[...], preferred_element_type=F32)
    rest = jnp.dot(left[:width, :], low[...], preferred_element_type=F32)
    acc[...] = both[:width, :] + both[width:, :] + rest
    half = acc.shape[0] // 2
    core = here[0] & 1
    keep[...] = acc[pl.ds(pl.multiple_of(core * half, 8), half), :]
    send[...] = acc[pl.ds(pl.multiple_of((1 - core) * half, 8), half), :]


def times(high, low, right, width):
    both = jnp.dot(high, right, preferred_element_type=F32)
    rest = jnp.dot(low, right[:, :width], preferred_element_type=F32)
    return both[:, :width] + both[:, width:] + rest


def products(group, size, high, low, right, out):
    for n, k in enumerate(group):
        at = pl.ds(k * size, size)
        value = times(high[at, :], low[at, :], right[...], right.shape[1] // 2)
        out[pl.ds(n * size, size), :] = value


def dense_kernel(
    blocks, group, size, here, high, low, mine, other, weight, bias, cotangent, *refs
):
    out, output, grads, piece_t, right, agg = refs
    width, total = agg.shape
    half, side = width // 2, total // blocks
    core = here[0] & 1
    agg[pl.ds(pl.multiple_of(core * half, 8), half), :] = mine[...]
    agg[pl.ds(pl.multiple_of((1 - core) * half, 8), half), :] = other[...]
    w = weight[...]
    for b in range(blocks):
        at = pl.ds(b * side, side)
        pre = dot3(agg[:, at].T, w) + bias[...]
        gate = jax.nn.sigmoid(pre)
        output[at, :] = pre * gate
        gradient = cotangent[at, :] * gate * (1.0 + pre * (1.0 - gate))
        grads[at, :] = gradient
        spread = dot3(gradient, w, (((1,), (1,)), ((), ())))
        upper, lower = halves(spread)
        right[at, :width] = upper.astype(BF16)
        right[at, width:] = lower.astype(BF16)
    products(group, size, high, low, right, out)
    piece = piece_t.shape[0]
    piece_t[...] = agg[pl.ds(pl.multiple_of(here[0] * piece, 8), piece), :]


def rest_kernel(groups, size, high, low, right, *outs):
    for group, out in zip(groups, outs):
        products(group, size, high, low, right, out)


def weight_kernel(piece_t, grads, out):
    piece, parts = piece_t.shape[0], grads.shape[1] // LANES
    g = grads[...]
    grad_weight = dot3(piece_t[...], g)
    grad_bias = jnp.sum(g, axis=0, keepdims=True)
    for q in range(parts):
        out[pl.ds(q * piece, piece), :] = grad_weight[:, q * LANES : (q + 1) * LANES]
    tail = [grad_bias[:, q * LANES : (q + 1) * LANES] for q in range(parts)]
    tail.append(jnp.zeros((PAD - parts, LANES), F32))
    out[pl.ds(parts * piece, PAD), :] = jnp.concatenate(tail, axis=0)


def add_kernel(cuts, count, *refs):
    mine, theirs, outs = refs[:count], refs[count : 2 * count], refs[2 * count :]
    for cut, out in zip(cuts, outs):
        to = 0
        for pair, first, second, rows in cut:
            left, right = pl.ds(first, rows), pl.ds(second, rows)
            out[pl.ds(to, rows), :] = mine[pair][left, :] + theirs[pair][right, :]
            to += rows


def add(mine, theirs, cuts=None):
    cuts = cuts or [[(n, 0, 0, x.shape[0])] for n, x in enumerate(mine)]
    total = sum(x.size for x in mine)
    return call(
        functools.partial(add_kernel, cuts, len(mine)),
        [(sum(cut[-1] for cut in cuts_of), mine[0].shape[1]) for cuts_of in cuts],
        [VMEM] * (2 * len(mine)),
        [],
        total,
        12 * total,
    )(*mine, *theirs)


def final_kernel(reps, blocks, part, piece, here, *refs):
    parts, weights = refs[:reps], refs[reps : 2 * reps]
    grad_features, grad_weight, grad_bias = refs[2 * reps :]
    side = grad_features.shape[0] // blocks
    groups = grad_weight.shape[1] // LANES
    for d in range(reps):
        q = here[0] ^ d
        for b in range(blocks):
            at = pl.ds(pl.multiple_of(b * side + q * part, 8), part)
            grad_features[at, :] = parts[d][pl.ds(b * part, part), :]
        at = pl.ds(pl.multiple_of(q * piece, 8), piece)
        for g in range(groups):
            grad_weight[at, pl.ds(g * LANES, LANES)] = weights[d][pl.ds(g * piece, piece), :]
    for g in range(groups):
        row = weights[0][pl.ds(groups * piece + g, 1), :]
        grad_bias[:, pl.ds(g * LANES, LANES)] = row


def per_device(features, weight, bias, tile_values, tile_rows, tile_cols, tile_count, cotangent):
    loops, reps = lax.axis_size("loop"), lax.axis_size("rep")
    slots, side = tile_values.shape[0], tile_values.shape[1]
    total, width = features.shape
    wide = weight.shape[1]
    blocks = total // side
    part, piece = side // reps, width // reps
    size, depth = blocks * part, loops * blocks * part
    extra = wide // LANES * piece + PAD
    here = lax.axis_index("rep").astype(jnp.int32).reshape(1)
    loop_at = lax.axis_index("loop").astype(jnp.int32).reshape(1)
    bias = bias.reshape(1, wide)

    def swap(x, axis, bit):
        pairs, low = [], min(loops, 4)
        for a in range(loops):
            for b in range(reps):
                turn = axis == "loop" and bit < low and not b & 1
                over = (2 * bit if 2 * bit < low else 1) if turn else bit
                to = (a ^ over, b) if axis == "loop" else (a, b ^ bit)
                pairs.append((a * reps + b, to[0] * reps + to[1]))
        return lax.ppermute(x, ("loop", "rep"), pairs)

    def join(*arrays):
        shape = (sum(x.shape[0] for x in arrays), arrays[0].shape[1])
        return call(
            join_kernel, [shape], [VMEM] * len(arrays), [], 0, 8 * shape[0] * shape[1]
        )(*arrays)[0]

    chunks = 4 if slots % 4 == 0 else 1
    sources = (features, tile_values, tile_rows[None], tile_cols[None])
    own, *parcels = call(
        functools.partial(pack_kernel, reps, loops, blocks, part),
        [(size, width)] + [(slots * part + PAD, side)] * reps,
        [SMEM] * 3 + [HBM] * 4,
        [
            pltpu.VMEM((slots, side, side), F32),
            pltpu.VMEM((slots, side, side), F32),
            pltpu.VMEM((1, slots), jnp.int32),
            pltpu.VMEM((1, slots), jnp.int32),
            pltpu.SemaphoreType.DMA((2 + chunks + blocks,)),
        ],
        0,
        2 * tile_values.size * 4,
    )(here, loop_at, tile_count, *[pltpu.with_memory_space_constraint(x, pltpu.HBM) for x in sources])
    tiles = [parcels[0]] + [swap(parcels[d], "rep", d) for d in range(1, reps)]

    bit = loops // 2
    feats, orders = [own, swap(own, "loop", bit)], [[0], [bit]]
    bit //= 2
    while bit > 1:
        order = sum(orders, [])
        far = [swap(x, "loop", bit) for x in feats]
        feats, orders = [join(*feats), join(*far)], [order, [k | bit for k in order]]
        bit //= 2
    feats += [swap(x, "loop", 1) for x in feats]
    orders += [[k | 1 for k in order] for order in orders]

    def scratch(count):
        return [
            pltpu.VMEM((count, PAD, LANES), jnp.int32),
            pltpu.SMEM((count, PAD, LANES), jnp.int32),
            pltpu.SemaphoreType.DMA,
        ]

    shapes = [(depth, total)] + [((depth, total), BF16)] * 2
    matrix = call(
        functools.partial(near_kernel, blocks, part, slots),
        shapes,
        [VMEM] * 2,
        scratch(2),
        0,
        8 << 20,
    )(*tiles[:2])
    _, high, low = call(
        functools.partial(far_kernel, blocks, part, slots, reps - 2),
        shapes,
        [VMEM] * (reps + 4),
        scratch(reps - 2),
        0,
        8 << 20,
        aliases={0: 0, 1: 1, 2: 2},
    )(*matrix, *tiles[2:], weight, bias, cotangent)

    send, keep = call(
        functools.partial(forward_kernel, orders),
        [(width // 2, total)] * 2,
        [SMEM] + [VMEM] * (2 + len(feats)),
        [pltpu.VMEM((2 * width, depth), BF16), pltpu.VMEM((width, total), F32)],
        2 * depth * total * width * 3,
        4 << 20,
    )(here, high, low, *feats)
    (mine,) = add([keep], [swap(send, "rep", 1)])
    bit = 2
    while bit < reps:
        (mine,) = add([mine], [swap(mine, "rep", bit)])
        bit *= 2
    other = swap(mine, "rep", 1)

    even = range(0, loops, 2)
    on, stay = [k for k in even if k & 2], [k for k in even if not k & 2]
    groups = [[k | 1 for k in on], [k | 1 for k in stay], on, stay]
    first, output, grads, piece_t, right = call(
        functools.partial(dense_kernel, blocks, groups[0], size),
        [(len(on) * size, width)]
        + [(total, wide)] * 2
        + [(piece, total), ((total, 2 * width), BF16)],
        [SMEM] + [VMEM] * 7,
        [pltpu.VMEM((width, total), F32)],
        2 * depth * total * width,
        4 << 20,
    )(here, high, low, mine, other, weight, bias, cotangent)
    on_term = swap(first, "loop", 1)
    sent, on_own, stay_own = call(
        functools.partial(rest_kernel, groups[1:], size),
        [(len(g) * size, width) for g in groups[1:]],
        [VMEM] * 3,
        [],
        2 * depth * total * width * 2,
        3 << 20,
    )(high, low, right)
    stay_term = swap(sent, "loop", 1)
    (grad,) = call(
        weight_kernel, [(extra, LANES)], [VMEM] * 2, [], 2 * piece * total * wide * 3, 1 << 20
    )(piece_t, grads)

    grad_term = swap(grad, "loop", loops // 2)
    (going,) = add([on_own], [on_term])
    term = swap(going, "loop", 2)
    (grad,) = add([grad], [grad_term])
    grad_term = swap(grad, "loop", 2)
    (held,) = add([stay_own], [stay_term])
    bit, rest = 2, stay
    while bit < loops // 2:
        ahead = [(0, n * size, n * size, size) for n, k in enumerate(rest) if k & (2 * bit)]
        behind = [(0, n * size, n * size, size) for n, k in enumerate(rest) if not k & (2 * bit)]
        rest = [k for k in rest if not k & (2 * bit)]
        going, held = add([held], [term], [ahead, behind])
        term = swap(going, "loop", 2 * bit)
        (grad,) = add([grad], [grad_term])
        grad_term = swap(grad, "loop", bit if bit > 2 else 1)
        bit *= 2
    (mine,) = add([held], [term])
    (grad,) = add([grad], [grad_term])

    def spread(own):
        found = {0: own}
        bit = reps // 2
        while bit:
            for k in list(found):
                found[k | bit] = swap(found[k], "rep", bit)
            bit //= 2
        return [found[d] for d in range(reps)]

    parts, weights = spread(mine), spread(grad)
    output = join(output)
    grad_features, grad_weight, grad_bias = call(
        functools.partial(final_kernel, reps, blocks, part, piece),
        [(total, width), (width, wide), (1, wide)],
        [SMEM] + [VMEM] * (2 * reps),
        [],
        0,
        2 * total * width * 4,
    )(here, *parts, *weights)
    return (output, grad_features, grad_weight, grad_bias.reshape(wide))


def solution(mesh):
    return jax.shard_map(
        per_device,
        mesh=mesh,
        in_specs=(
            P("loop", None),
            P(),
            P(),
            P(("loop", "rep"), None, None),
            P(("loop", "rep")),
            P(("loop", "rep")),
            P(("loop", "rep")),
            P("loop", None),
        ),
        out_specs=(P("loop", None), P("loop", None), P(), P()),
        check_vma=False,
    )
```

```python
import functools

import jax
import jax.numpy as jnp
from jax import lax
from jax.experimental import pallas as pl
from jax.experimental.pallas import tpu as pltpu
from jax.sharding import PartitionSpec as P


LANES = 128
PAD = 8
F32 = jnp.float32
BF16 = jnp.bfloat16
VMEM = pl.BlockSpec(memory_space=pltpu.VMEM)
SMEM = pl.BlockSpec(memory_space=pltpu.SMEM)
HBM = pl.BlockSpec(memory_space=pltpu.HBM)


def halves(x):
    high = x.astype(BF16).astype(F32)
    return high, x - high


def dot3(a, b, dims=(((1,), (0,)), ((), ()))):
    ah, al = halves(a)
    bh, bl = halves(b)
    ah, al, bh, bl = (v.astype(BF16) for v in (ah, al, bh, bl))
    dot = functools.partial(lax.dot_general, dimension_numbers=dims, preferred_element_type=F32)
    return dot(ah, bh) + dot(ah, bl) + dot(al, bh)


def call(kernel, out_shapes, in_specs, scratch, flops, moved, limit=24, aliases=None):
    return pl.pallas_call(
        kernel,
        input_output_aliases=aliases or {},
        out_shape=[
            jax.ShapeDtypeStruct(*(s if isinstance(s[0], tuple) else (s, F32))) for s in out_shapes
        ],
        in_specs=in_specs,
        out_specs=[VMEM] * len(out_shapes),
        scratch_shapes=scratch,
        compiler_params=pltpu.CompilerParams(vmem_limit_bytes=limit << 20),
        cost_estimate=pl.CostEstimate(flops=flops, bytes_accessed=moved, transcendentals=0),
    )


def join_kernel(*refs):
    at = 0
    for ref in refs[:-1]:
        refs[-1][pl.ds(at, ref.shape[0]), :] = ref[...]
        at += ref.shape[0]


def pack_kernel(reps, loops, blocks, part, rep_at, at_loop, count, features, tiles, rows, cols, *refs):
    own, outs = refs[0], refs[1 : 1 + reps]
    held, turned, row_ids, col_ids, sem = refs[1 + reps :]
    here, loop_at = rep_at[0], at_loop[0]
    slots, side = tiles.shape[0], tiles.shape[1]
    chunks = sem.shape[0] - 2 - blocks
    step = slots // chunks
    small = [
        pltpu.make_async_copy(source, target, sem.at[n])
        for n, (source, target) in enumerate([(rows, row_ids), (cols, col_ids)])
    ]
    large = [
        pltpu.make_async_copy(
            tiles.at[pl.ds(n * step, step)], held.at[pl.ds(n * step, step)], sem.at[2 + n]
        )
        for n in range(chunks)
    ]
    pieces = [
        pltpu.make_async_copy(
            features.at[pl.ds(pl.multiple_of(b * side + here * part, 8), part), :],
            own.at[pl.ds(b * part, part), :],
            sem.at[2 + chunks + b],
        )
        for b in range(blocks)
    ]
    for copy in small + large + pieces:
        copy.start()
    for copy in small:
        copy.wait()
    local_rows = row_ids[...] - loop_at * blocks
    shift = blocks.bit_length() - 1
    away = (col_ids[...] >> shift) ^ loop_at
    low = min(loops, 4) - 1
    other_way = (away & ~low) | ((away & low) >> 1) | jnp.where(away & 1 == 1, (low + 1) // 2, 0)
    for d in range(reps):
        second = ((here ^ d) & 1) * jnp.ones_like(away)
        order = jnp.where(second == 1, away, other_way)
        column = (order << shift) | (col_ids[...] & (blocks - 1))
        meta = jnp.concatenate([local_rows, column], axis=0).astype(F32)
        outs[d][pl.ds(slots * part, 2), pl.ds(0, slots)] = meta
    alive = count[0]
    for n in range(chunks):
        large[n].wait()
        for s in range(n * step, (n + 1) * step):
            turned[s] = jnp.where(s < alive, held[s].T, jnp.zeros((side, side), F32))
            for d in range(reps):
                start = pl.multiple_of((here ^ d) * part, 8)
                outs[d][pl.ds(s * part, part), :] = turned[s, pl.ds(start, part), :]
    for copy in pieces:
        copy.wait()


def place_parts(blocks, part, slots, tiles, dense, place_vector, place, sem, clear, both=()):
    side = dense.shape[1] // blocks
    for d, tile in enumerate(tiles):
        place_vector[d] = tile[pl.ds(slots * part, PAD), :].astype(jnp.int32)
    copy = pltpu.make_async_copy(place_vector, place, sem)
    copy.start()
    if clear:
        dense[...] = jnp.zeros_like(dense)
    copy.wait()
    for d, tile in enumerate(tiles):
        for s in range(slots):
            lane = pl.ds(pl.multiple_of(place[d, 0, s] * side, LANES), side)
            at = pl.ds(pl.multiple_of(place[d, 1, s] * part, part), part)
            value = dense[at, lane] + tile[pl.ds(s * part, part), :]
            dense[at, lane] = value
            for ref, term in zip(both, halves(value)):
                ref[at, lane] = term.astype(BF16)


def split(dense, high_out, low_out):
    side = 8 * 16
    for k in range(dense.shape[0] // side):
        at = pl.ds(k * side, side)
        high, low = halves(dense[at, :])
        high_out[at, :] = high.astype(BF16)
        low_out[at, :] = low.astype(BF16)


def near_kernel(blocks, part, slots, *refs):
    dense, high_out, low_out = refs[-6:-3]
    place_parts(blocks, part, slots, refs[:-6], dense, *refs[-3:], True)
    split(dense, high_out, low_out)


def far_kernel(blocks, part, slots, count, *refs):
    tiles = refs[3 : 3 + count]
    dense, high_out, low_out = refs[-6:-3]
    both = (high_out, low_out) if part % 16 == 0 else ()
    place_parts(blocks, part, slots, tiles, dense, *refs[-3:], False, both)
    if not both:
        split(dense, high_out, low_out)


def forward_kernel(orders, here, high, low, *refs):
    feats = refs[: len(orders)]
    send, keep, left, acc = refs[len(orders) :]
    width = left.shape[0] // 2
    for order, feat in zip(orders, feats):
        rows = feat.shape[0] // len(order)
        for n, k in enumerate(order):
            at = pl.ds(k * rows, rows)
            upper, lower = halves(feat[pl.ds(n * rows, rows), :].T)
            left[:width, at] = upper.astype(BF16)
            left[width:, at] = lower.astype(BF16)
    both = jnp.dot(left[...], high[...], preferred_element_type=F32)
    rest = jnp.dot(left[:width, :], low[...], preferred_element_type=F32)
    acc[...] = both[:width, :] + both[width:, :] + rest
    half = acc.shape[0] // 2
    core = here[0] & 1
    keep[...] = acc[pl.ds(pl.multiple_of(core * half, 8), half), :]
    send[...] = acc[pl.ds(pl.multiple_of((1 - core) * half, 8), half), :]


def times(high, low, right, width):
    both = jnp.dot(high, right, preferred_element_type=F32)
    rest = jnp.dot(low, right[:, :width], preferred_element_type=F32)
    return both[:, :width] + both[:, width:] + rest


def products(group, size, high, low, right, out):
    for n, k in enumerate(group):
        at = pl.ds(k * size, size)
        value = times(high[at, :], low[at, :], right[...], right.shape[1] // 2)
        out[pl.ds(n * size, size), :] = value


def dense_kernel(
    blocks, group, size, here, high, low, mine, other, weight, bias, cotangent, *refs
):
    out, output, grads, piece_t, right, agg = refs
    width, total = agg.shape
    half, side = width // 2, total // blocks
    core = here[0] & 1
    agg[pl.ds(pl.multiple_of(core * half, 8), half), :] = mine[...]
    agg[pl.ds(pl.multiple_of((1 - core) * half, 8), half), :] = other[...]
    w = weight[...]
    for b in range(blocks):
        at = pl.ds(b * side, side)
        pre = dot3(agg[:, at].T, w) + bias[...]
        gate = jax.nn.sigmoid(pre)
        output[at, :] = pre * gate
        gradient = cotangent[at, :] * gate * (1.0 + pre * (1.0 - gate))
        grads[at, :] = gradient
        spread = dot3(gradient, w, (((1,), (1,)), ((), ())))
        upper, lower = halves(spread)
        right[at, :width] = upper.astype(BF16)
        right[at, width:] = lower.astype(BF16)
    products(group, size, high, low, right, out)
    piece = piece_t.shape[0]
    piece_t[...] = agg[pl.ds(pl.multiple_of(here[0] * piece, 8), piece), :]


def rest_kernel(groups, size, high, low, right, *outs):
    for group, out in zip(groups, outs):
        products(group, size, high, low, right, out)


def weight_kernel(piece_t, grads, out):
    piece, parts = piece_t.shape[0], grads.shape[1] // LANES
    g = grads[...]
    grad_weight = dot3(piece_t[...], g)
    grad_bias = jnp.sum(g, axis=0, keepdims=True)
    for q in range(parts):
        out[pl.ds(q * piece, piece), :] = grad_weight[:, q * LANES : (q + 1) * LANES]
    tail = [grad_bias[:, q * LANES : (q + 1) * LANES] for q in range(parts)]
    tail.append(jnp.zeros((PAD - parts, LANES), F32))
    out[pl.ds(parts * piece, PAD), :] = jnp.concatenate(tail, axis=0)


def add_kernel(cuts, count, *refs):
    mine, theirs, outs = refs[:count], refs[count : 2 * count], refs[2 * count :]
    for cut, out in zip(cuts, outs):
        to = 0
        for pair, first, second, rows in cut:
            left, right = pl.ds(first, rows), pl.ds(second, rows)
            out[pl.ds(to, rows), :] = mine[pair][left, :] + theirs[pair][right, :]
            to += rows


def add(mine, theirs, cuts=None):
    cuts = cuts or [[(n, 0, 0, x.shape[0])] for n, x in enumerate(mine)]
    total = sum(x.size for x in mine)
    return call(
        functools.partial(add_kernel, cuts, len(mine)),
        [(sum(cut[-1] for cut in cuts_of), mine[0].shape[1]) for cuts_of in cuts],
        [VMEM] * (2 * len(mine)),
        [],
        total,
        12 * total,
    )(*mine, *theirs)


def features_kernel(reps, blocks, part, here, *refs):
    grad_features = refs[reps]
    side = grad_features.shape[0] // blocks
    for d in range(reps):
        for b in range(blocks):
            at = pl.ds(pl.multiple_of(b * side + (here[0] ^ d) * part, 8), part)
            grad_features[at, :] = refs[d][pl.ds(b * part, part), :]


def weights_kernel(reps, piece, here, *refs):
    grad_weight, grad_bias = refs[reps:]
    groups = grad_weight.shape[1] // LANES
    for g in range(groups):
        lane = pl.ds(g * LANES, LANES)
        for d in range(reps):
            at = pl.ds(pl.multiple_of((here[0] ^ d) * piece, 8), piece)
            grad_weight[at, lane] = refs[d][pl.ds(g * piece, piece), :]
        grad_bias[:, lane] = refs[0][pl.ds(groups * piece + g, 1), :]


def per_device(features, weight, bias, tile_values, tile_rows, tile_cols, tile_count, cotangent):
    loops, reps = lax.axis_size("loop"), lax.axis_size("rep")
    slots, side = tile_values.shape[0], tile_values.shape[1]
    total, width = features.shape
    wide = weight.shape[1]
    blocks = total // side
    part, piece = side // reps, width // reps
    size, depth = blocks * part, loops * blocks * part
    extra = wide // LANES * piece + PAD
    here = lax.axis_index("rep").astype(jnp.int32).reshape(1)
    loop_at = lax.axis_index("loop").astype(jnp.int32).reshape(1)
    bias = bias.reshape(1, wide)

    def swap(x, axis, bit):
        pairs, low = [], min(loops, 4)
        for a in range(loops):
            for b in range(reps):
                turn = axis == "loop" and bit < low and not b & 1
                over = (2 * bit if 2 * bit < low else 1) if turn else bit
                to = (a ^ over, b) if axis == "loop" else (a, b ^ bit)
                pairs.append((a * reps + b, to[0] * reps + to[1]))
        return lax.ppermute(x, ("loop", "rep"), pairs)

    def join(*arrays):
        shape = (sum(x.shape[0] for x in arrays), arrays[0].shape[1])
        return call(
            join_kernel, [shape], [VMEM] * len(arrays), [], 0, 8 * shape[0] * shape[1]
        )(*arrays)[0]

    chunks = 8 if slots % 8 == 0 else 1
    sources = (features, tile_values, tile_rows[None], tile_cols[None])
    own, *parcels = call(
        functools.partial(pack_kernel, reps, loops, blocks, part),
        [(size, width)] + [(slots * part + PAD, side)] * reps,
        [SMEM] * 3 + [HBM] * 4,
        [
            pltpu.VMEM((slots, side, side), F32),
            pltpu.VMEM((slots, side, side), F32),
            pltpu.VMEM((1, slots), jnp.int32),
            pltpu.VMEM((1, slots), jnp.int32),
            pltpu.SemaphoreType.DMA((2 + chunks + blocks,)),
        ],
        0,
        2 * tile_values.size * 4,
    )(here, loop_at, tile_count, *[pltpu.with_memory_space_constraint(x, pltpu.HBM) for x in sources])
    tiles = [parcels[0]] + [swap(parcels[d], "rep", d) for d in range(1, reps)]

    bit = loops // 2
    feats, orders = [own, swap(own, "loop", bit)], [[0], [bit]]
    bit //= 2
    while bit > 1:
        order = sum(orders, [])
        far = [swap(x, "loop", bit) for x in feats]
        feats, orders = [join(*feats), join(*far)], [order, [k | bit for k in order]]
        bit //= 2
    feats += [swap(x, "loop", 1) for x in feats]
    orders += [[k | 1 for k in order] for order in orders]

    def scratch(count):
        return [
            pltpu.VMEM((count, PAD, LANES), jnp.int32),
            pltpu.SMEM((count, PAD, LANES), jnp.int32),
            pltpu.SemaphoreType.DMA,
        ]

    shapes = [(depth, total)] + [((depth, total), BF16)] * 2
    matrix = call(
        functools.partial(near_kernel, blocks, part, slots),
        shapes,
        [VMEM] * 2,
        scratch(2),
        0,
        8 << 20,
    )(*tiles[:2])
    _, high, low = call(
        functools.partial(far_kernel, blocks, part, slots, reps - 2),
        shapes,
        [VMEM] * (reps + 4),
        scratch(reps - 2),
        0,
        8 << 20,
        aliases={0: 0, 1: 1, 2: 2},
    )(*matrix, *tiles[2:], weight, bias, cotangent)

    send, keep = call(
        functools.partial(forward_kernel, orders),
        [(width // 2, total)] * 2,
        [SMEM] + [VMEM] * (2 + len(feats)),
        [pltpu.VMEM((2 * width, depth), BF16), pltpu.VMEM((width, total), F32)],
        2 * depth * total * width * 3,
        4 << 20,
    )(here, high, low, *feats)
    (mine,) = add([keep], [swap(send, "rep", 1)])
    bit = 2
    while bit < reps:
        (mine,) = add([mine], [swap(mine, "rep", bit)])
        bit *= 2
    other = swap(mine, "rep", 1)

    even = range(0, loops, 2)
    on, stay = [k for k in even if k & 2], [k for k in even if not k & 2]
    on.sort(key=lambda k: (not k & 4, k))
    stay.sort(key=lambda k: (not k & 4, k))
    groups = [[k | 1 for k in on], [k | 1 for k in stay], on, stay]
    first, output, grads, piece_t, right = call(
        functools.partial(dense_kernel, blocks, groups[0], size),
        [(len(on) * size, width)]
        + [(total, wide)] * 2
        + [(piece, total), ((total, 2 * width), BF16)],
        [SMEM] + [VMEM] * 7,
        [pltpu.VMEM((width, total), F32)],
        2 * depth * total * width,
        4 << 20,
    )(here, high, low, mine, other, weight, bias, cotangent)
    on_term = swap(first, "loop", 1)
    sent, on_own, stay_own = call(
        functools.partial(rest_kernel, groups[1:], size),
        [(len(g) * size, width) for g in groups[1:]],
        [VMEM] * 3,
        [],
        2 * depth * total * width * 2,
        3 << 20,
    )(high, low, right)
    stay_term = swap(sent, "loop", 1)
    (grad,) = call(
        weight_kernel, [(extra, LANES)], [VMEM] * 2, [], 2 * piece * total * wide * 3, 1 << 20
    )(piece_t, grads)

    grad_term = swap(grad, "loop", loops // 2)
    cut = size * sum(1 for k in on if k & 4)
    cuts = [[(0, 0, 0, cut)], [(0, cut, cut, len(on) * size - cut)]]
    going, later = add([on_own], [on_term], cuts)
    term = swap(going, "loop", 2)
    later_term = swap(later, "loop", 2)
    (grad,) = add([grad], [grad_term])
    grad_term = swap(grad, "loop", 2)
    going, held = add([stay_own], [stay_term], cuts)
    (going,) = add([going], [term])
    term = swap(going, "loop", 4)
    (held,) = add([held], [later_term])
    (grad,) = add([grad], [grad_term])
    grad_term = swap(grad, "loop", 1)
    bit, rest = 4, [k for k in stay if not k & 4]
    while bit < loops // 2:
        ahead = [(0, n * size, n * size, size) for n, k in enumerate(rest) if k & (2 * bit)]
        behind = [(0, n * size, n * size, size) for n, k in enumerate(rest) if not k & (2 * bit)]
        rest = [k for k in rest if not k & (2 * bit)]
        going, held = add([held], [term], [ahead, behind])
        term = swap(going, "loop", 2 * bit)
        (grad,) = add([grad], [grad_term])
        grad_term = swap(grad, "loop", bit)
        bit *= 2
    (mine,) = add([held], [term])
    (grad,) = add([grad], [grad_term])

    def spread(own):
        found = {0: own}
        bit = reps // 2
        while bit:
            for k in list(found):
                found[k | bit] = swap(found[k], "rep", bit)
            bit //= 2
        return [found[d] for d in range(reps)]

    parts, weights = spread(mine), spread(grad)
    output = join(output)
    (grad_features,) = call(
        functools.partial(features_kernel, reps, blocks, part),
        [(total, width)],
        [SMEM] + [VMEM] * reps,
        [],
        0,
        2 * total * width * 4,
    )(here, *parts)
    grad_weight, grad_bias = call(
        functools.partial(weights_kernel, reps, piece),
        [(width, wide), (1, wide)],
        [SMEM] + [VMEM] * reps,
        [],
        0,
        2 * width * wide * 4,
    )(here, *weights)
    return (output, grad_features, grad_weight, grad_bias.reshape(wide))


def solution(mesh):
    return jax.shard_map(
        per_device,
        mesh=mesh,
        in_specs=(
            P("loop", None),
            P(),
            P(),
            P(("loop", "rep"), None, None),
            P(("loop", "rep")),
            P(("loop", "rep")),
            P(("loop", "rep")),
            P("loop", None),
        ),
        out_specs=(P("loop", None), P("loop", None), P(), P()),
        check_vma=False,
    )
```
